256 devices in a mesh: tm: 16 (over y, x_hi, core), fsdp: 16 (over x_lo, z).
Axes of the slice: x: 4 (x_hi: 2, x_lo: 2; x = x_hi * 2 + x_lo), y: 4, z: 8, core: 2. Of those that a mesh axis runs over, the one named last changes fastest.
Arguments:
- stacked_mels: bfloat16 [16, 12288, 512], P('fsdp', 'tm'), may hold values from -6 to 6
- utt_lengths: int32 [16, 64], P('fsdp'), may hold values from 1 to 1536, 12288 in all within a row
- sub_weight: bfloat16 [512, 1536], P('fsdp'), may hold values from -0.25 to 0.25
- norm_gain: float32 [1536], replicated, may hold values from 0.1 to 1.9
- first_weight: bfloat16 [1536, 3072], P('fsdp'), may hold values from -0.15625 to 0.15625
- dw_kernel: bfloat16 [32, 1536], replicated, may hold values from -1 to 1
- bn_scale: float32 [1536], replicated, may hold values from 0.5 to 2
- second_weight: bfloat16 [1536, 1536], P('fsdp'), may hold values from -0.15625 to 0.15625
Outputs:
- encoded: bfloat16 [16, 12288, 1536], P('fsdp', 'tm')
The draws below stay inside these ranges and needn't reach their ends.
Inputs may be any that keep to these rules, and one draw needn't show every extreme that they name: `utt_lengths`: each row sums to 12288; the longest utterance of every row has exactly 1536 frames.
All inputs are finite; a program needn't handle non-finite values.
Results may differ from the reference program's by a relative error of at most 0.008.
Values may be sent and summed in bfloat16 or wider, within the bound.
No kernel may reach another device: no remote copies, remote signals or barrier semaphores. Data moves between devices by JAX's collectives and lax.ppermute only.
A program may use at most 128 MiB of HBM per device.

```python
import math
import jax
import jax.numpy as jnp
import numpy as np
from jax import lax

D = 1536
MELS = 128
SUB = 4
KW = 32
FRAMES = 12288
SEQS = 16
UTTS = 64
UTT_MOST = 1536


def shard_levels(own_key, dims, cuts, low, top_value):
    factor_of = 1.0
    for axis_at, parts in cuts:
        steps = jax.random.uniform(jax.random.fold_in(jax.random.fold_in(own_key, 6), axis_at), (parts,), jnp.float32, low / len(cuts), top_value / len(cuts))
        factor_of = factor_of * jnp.repeat(jnp.exp(steps), dims[axis_at] // parts).reshape((-1,) + (1,) * (len(dims) - 1 - axis_at))
    return factor_of


def profile(number_of, total, most, slope):
    portions = [(1 << 20) // math.isqrt(grade ** slope) + 1 for grade in range(2, number_of + 1)]
    surplus, holding = total - most - (number_of - 1), [1] * (number_of - 1)
    while surplus > 0:
        movable = [i for i in range(number_of - 1) if holding[i] < most]
        mass, remaining = sum([portions[i] for i in movable]), surplus
        for i in movable:
            addition = min(most - holding[i], max(1, remaining * portions[i] // mass), surplus)
            holding[i] = holding[i] + addition
            surplus = surplus - addition
    return np.array([most] + holding)


def uneven_parts(own_key, amount, total, most, skew):
    if amount == 2:
        one = jax.random.randint(own_key, (), max(1, total - most), min(most, total - 1) + 1)
        return jnp.stack([one, total - one])
    tallies = jnp.asarray(profile(amount, total, most, skew), jnp.int32)
    pairs = (amount - 1) // 2
    source_of, taker = tallies[1:1 + 2 * pairs:2], tallies[2:2 + 2 * pairs:2]
    slack = jnp.minimum(source_of - 1, most - taker)
    shifted = jax.random.randint(jax.random.fold_in(own_key, 1), (pairs,), 0, 1 << 20) % (slack + 1)
    tallies = tallies.at[1:1 + 2 * pairs:2].set(source_of - shifted).at[2:2 + 2 * pairs:2].set(taker + shifted)
    return tallies[jax.random.permutation(jax.random.fold_in(own_key, 2), amount)]


def noise(key, dims, scale, bound, shards=(), held_as=jnp.bfloat16):
    array = scale * jax.random.normal(key, dims, jnp.float32)
    if shards:
        array = array * shard_levels(key, dims, shards, -0.22, 0.18)
    return jnp.clip(array, -bound, bound).astype(held_as)


def setup_inputs(seed: int = 0) -> dict:
    streams_of = jax.random.split(jax.random.key(seed), 9)
    return {
        "stacked_mels": noise(streams_of[0], (SEQS, FRAMES, SUB * MELS), 1.0, 6.0, ((0, 16), (1, 16))),
        "utt_lengths": jax.vmap(lambda own: uneven_parts(own, UTTS, FRAMES, UTT_MOST, 2))(jax.random.split(streams_of[1], SEQS)).reshape((SEQS, UTTS)).astype(jnp.int32),
        "sub_weight": noise(streams_of[2], (SUB * MELS, D), (SUB * MELS) ** -0.5, 0.25, ((0, 16),)),
        "norm_gain": jnp.clip(1.0 + 0.18 * jax.random.normal(streams_of[3], (D,), jnp.float32), 0.1, 1.9),
        "first_weight": noise(streams_of[4], (D, 2 * D), D ** -0.5, 0.15625, ((0, 16),)),
        "dw_kernel": noise(streams_of[5], (KW, D), KW ** -0.5, 1.0),
        "bn_scale": jnp.clip(jnp.exp(jax.random.uniform(streams_of[6], (D,), jnp.float32, math.log(0.5), math.log(2.0))), 0.5, 2.0),
        "second_weight": noise(streams_of[7], (D, D), D ** -0.5, 0.15625, ((0, 16),)),
    }


def frame_ids(lengths, positions):
    ends = jnp.cumsum(lengths)
    return lax.optimization_barrier(jnp.sum((positions[:, None] >= ends[None, :]).astype(jnp.int32), axis=1))

def one_sequence(stacked, lengths, sub_weight, norm_gain, first_weight, dw_kernel, bn_scale, second_weight):
    sub = jnp.dot(stacked, sub_weight, preferred_element_type=jnp.float32).astype(jnp.bfloat16)
    subf = sub.astype(jnp.float32)
    mean = lax.optimization_barrier(jnp.mean(subf, axis=1, keepdims=True))
    var = lax.optimization_barrier(jnp.mean((subf - mean) ** 2, axis=1, keepdims=True))
    normed = ((subf - mean) * lax.rsqrt(var + 1e-05) * norm_gain).astype(jnp.bfloat16)
    proj = jnp.dot(normed, first_weight, preferred_element_type=jnp.float32)
    width = sub.shape[1]
    glu = (proj[:, :width] * jax.nn.sigmoid(proj[:, width:])).astype(jnp.bfloat16)
    frames = stacked.shape[0]
    positions = jnp.arange(frames, dtype=jnp.int32)
    ids = frame_ids(lengths, positions)
    half = KW // 2
    padded = jnp.pad(glu.astype(jnp.float32), ((half, half), (0, 0)))
    padded_ids = jnp.pad(ids, (half, half), constant_values=-1)
    depth = jnp.zeros((frames, width), jnp.float32)
    for k in range(KW):
        same = padded_ids[k:k + frames] == ids
        depth = depth + jnp.where(same[:, None], padded[k:k + frames] * dw_kernel[k].astype(jnp.float32), 0.0)
    scaled = depth * bn_scale
    act = (scaled * jax.nn.sigmoid(scaled)).astype(jnp.bfloat16)
    return (subf + jnp.dot(act, second_weight, preferred_element_type=jnp.float32)).astype(jnp.bfloat16)

def reference(stacked_mels, utt_lengths, sub_weight, norm_gain, first_weight, dw_kernel, bn_scale, second_weight):

    def apply(pair):
        return one_sequence(pair[0], pair[1], sub_weight, norm_gain, first_weight, dw_kernel, bn_scale, second_weight)
    return lax.map(apply, (stacked_mels, utt_lengths))
```

```python
import functools

import jax
import jax.numpy as jnp
from jax import lax
from jax.experimental import pallas as pl
from jax.experimental.pallas import tpu as pltpu
from jax.sharding import Mesh
from jax.sharding import PartitionSpec as P

KW = 32
HALF = KW // 2
TM = ("y", "xh", "c")
FS = ("xl", "z")
X = ("xh", "xl")
TILE = 32
ANY = pl.BlockSpec(memory_space=pl.ANY)
VM = pl.BlockSpec(memory_space=pltpu.VMEM)
SM = pl.BlockSpec(memory_space=pltpu.SMEM)


def cyc(n, s):
    return [(i, (i + s) % n) for i in range(n)]


def front_kernel(places, meta, ids_s, *refs):
    n = len(places)
    own, halo, recv = refs[:3]
    blocks = refs[3 : 3 + n]
    gain, taps, scale, ids_v, sub_out, act_own, act_send = refs[3 + n : 10 + n]
    mels, ws, wf, sub, normed, xs, idb, tmp, act, sem_in, sem_out = refs[10 + n :]
    c, z, xl = meta[0], meta[1], meta[2]
    span = own.shape[0]
    rows = mels.shape[0]
    width = sub.shape[1]
    hw = act.shape[1]
    sr = ws.shape[0] // 16
    fr = wf.shape[0] // 16

    mine = pl.multiple_of(HALF + span * c, HALF)
    other = pl.multiple_of(HALF + span * (1 - c), HALF)
    outer = pl.multiple_of((rows - HALF) * c, HALF)
    inner = pl.multiple_of((rows - HALF) * (1 - c), HALF)
    copies = [
        pltpu.make_async_copy(own, mels.at[pl.ds(mine, span)], sem_in.at[0]),
        pltpu.make_async_copy(recv.at[pl.ds(0, span)], mels.at[pl.ds(other, span)], sem_in.at[1]),
        pltpu.make_async_copy(halo, mels.at[pl.ds(outer, HALF)], sem_in.at[2]),
        pltpu.make_async_copy(recv.at[pl.ds(span, HALF)], mels.at[pl.ds(inner, HALF)], sem_in.at[3]),
    ]
    late = []
    at = 4
    for (flip, shift, lo, hi), block in zip(places, blocks):
        xx = (1 - xl) if flip else xl
        j = xx * 8 + lax.rem(z + shift + 8, 8)
        if lo < sr:
            copies.append(
                pltpu.make_async_copy(
                    block.at[pl.ds(0, sr)],
                    ws.at[pl.ds(pl.multiple_of(j * sr, sr), sr)],
                    sem_in.at[at],
                )
            )
            at += 1
        a, b = max(lo, sr), hi
        late.append(
            pltpu.make_async_copy(
                block.at[pl.ds(a - lo, b - a)],
                wf.at[pl.ds(pl.multiple_of(j * fr + (a - sr), 32), b - a)],
                sem_in.at[at],
            )
        )
        at += 1
    for cp in copies + late:
        cp.start()
    idb[...] = jnp.broadcast_to(ids_v[...], idb.shape)
    for cp in copies:
        cp.wait()

    nb = 112

    def front(i, _):
        r = pl.ds(pl.multiple_of(i * nb, 16), nb)
        s = jnp.dot(mels[r, :], ws[...], preferred_element_type=jnp.float32).astype(jnp.bfloat16)
        sub[r, :] = s
        f = s.astype(jnp.float32)
        mean = jnp.sum(f, axis=1, keepdims=True) * (1.0 / width)
        d = f - mean
        var = jnp.sum(d * d, axis=1, keepdims=True) * (1.0 / width)
        normed[r, :] = (d * lax.rsqrt(var + 1e-05) * gain[...]).astype(jnp.bfloat16)
        return 0

    lax.fori_loop(0, rows // nb, front, 0)
    out_sub = pltpu.make_async_copy(sub.at[pl.ds(mine, span)], sub_out, sem_out.at[0])
    out_sub.start()
    for cp in late:
        cp.wait()

    mb = 224
    for cg in range(hw // 256):
        vcol, gcol = cg * 256, hw + cg * 256

        def gated(i, _):
            r = pl.ds(pl.multiple_of(i * mb, 16), mb)
            lhs = normed[r, :]
            v = jnp.dot(lhs, wf[:, vcol : vcol + 256], preferred_element_type=jnp.float32)
            g = jnp.dot(lhs, wf[:, gcol : gcol + 256], preferred_element_type=jnp.float32)
            glu = (v * jax.nn.sigmoid(g)).astype(jnp.bfloat16).astype(jnp.float32)
            xs[2 * cg, r, :] = glu[:, :128]
            xs[2 * cg + 1, r, :] = glu[:, 128:]
            return 0

        lax.fori_loop(0, rows // mb, gated, 0)

        for g in (2 * cg, 2 * cg + 1):

            def tile(i, _):
                t0 = pl.multiple_of(i * TILE, TILE)
                win = TILE + KW
                idw = idb[pl.ds(t0, win), :]
                ido = idb[pl.ds(pl.multiple_of(t0 + HALF, HALF), TILE), :]
                first = ids_s[t0 + HALF]
                last = ids_s[t0 + HALF + TILE - 1]

                def one(u, acc):
                    tmp[...] = jnp.where(idw == u, xs[g, pl.ds(t0, win), :], 0.0)
                    s = tmp[0:TILE, :] * taps[g, 0:1, :]
                    for k in range(1, KW):
                        s = s + tmp[k : k + TILE, :] * taps[g, k : k + 1, :]
                    return jnp.where(ido == u, s, acc)

                acc = lax.fori_loop(first, last + 1, one, jnp.zeros((TILE, 128), jnp.float32))
                u = acc * scale[:, g * 128 : (g + 1) * 128]
                act[pl.ds(t0, TILE), g * 128 : (g + 1) * 128] = (u * jax.nn.sigmoid(u)).astype(
                    jnp.bfloat16
                )
                return 0

            lax.fori_loop(0, 2 * span // TILE, tile, 0)

    outs = [
        pltpu.make_async_copy(
            act.at[pl.ds(pl.multiple_of(span * c, span), span)], act_own, sem_out.at[1]
        ),
        pltpu.make_async_copy(
            act.at[pl.ds(pl.multiple_of(span * (1 - c), span), span)], act_send, sem_out.at[2]
        ),
    ]
    for cp in outs:
        cp.start()
    out_sub.wait()
    for cp in outs:
        cp.wait()


def back_kernel(meta, sub, mine, theirs, w_mine, w_theirs, out, sub_v, a_v, w_v, o_v, sem_in, sem_out):
    c = meta[0]
    span, width = sub.shape
    hw = mine.shape[1]
    here = pl.multiple_of(hw * c, 128)
    there = pl.multiple_of(hw * (1 - c), 128)
    copies = [
        pltpu.make_async_copy(sub, sub_v, sem_in.at[0]),
        pltpu.make_async_copy(mine, a_v.at[:, pl.ds(here, hw)], sem_in.at[1]),
        pltpu.make_async_copy(theirs, a_v.at[:, pl.ds(there, hw)], sem_in.at[2]),
        pltpu.make_async_copy(w_mine, w_v.at[:, pl.ds(here, hw)], sem_in.at[3]),
        pltpu.make_async_copy(w_theirs, w_v.at[:, pl.ds(there, hw)], sem_in.at[4]),
    ]
    for cp in copies:
        cp.start()
    for cp in copies:
        cp.wait()
    nb = 192
    outs = []
    for i in range(span // nb):
        r = pl.ds(i * nb, nb)
        for n in range(0, width, 512):
            y = jnp.dot(a_v[r, :], w_v[:, n : n + 512], preferred_element_type=jnp.float32)
            o_v[r, n : n + 512] = (sub_v[r, n : n + 512].astype(jnp.float32) + y).astype(
                jnp.bfloat16
            )
        outs.append(pltpu.make_async_copy(o_v.at[r], out.at[r], sem_out.at[i]))
        outs[-1].start()
    for cp in outs:
        cp.wait()


def on_device(mels, utt_lengths, sub_weight, norm_gain, first_weight, dw_kernel, bn_scale, second_weight):
    _, span, stack = mels.shape
    width = second_weight.shape[1]
    hw = width // 2
    sr, fr = sub_weight.shape[0], first_weight.shape[0]
    c = lax.axis_index("c")
    z = lax.axis_index("z")
    xl = lax.axis_index("xl")
    chip = lax.axis_index("y") * 2 + lax.axis_index("xh")
    zp = lambda a: lax.ppermute(a, "z", cyc(8, 1))
    zm = lambda a: lax.ppermute(a, "z", cyc(8, -1))
    xp = lambda a: lax.ppermute(a, X, cyc(4, 1))
    xm = lambda a: lax.ppermute(a, X, cyc(4, -1))
    swap = lambda a: lax.ppermute(a, "c", cyc(2, 1))

    half = lambda a, at: lax.dynamic_slice_in_dim(a, at + c * hw, hw, axis=a.ndim - 1)
    block = jnp.concatenate(
        [sub_weight, jnp.concatenate([half(first_weight, 0), half(first_weight, width)], axis=1)]
    )
    hi = sr + fr
    mid = hi // 2
    places = [(False, 0, 0, hi), (True, 0, 0, hi)]
    blocks = [block, xp(block)]
    p = m = block
    for s in (1, 2, 3):
        p, m = zp(p), zm(m)
        blocks += [p, m, xp(p), xm(m)]
        places += [(False, -s, 0, hi), (False, s, 0, hi), (True, -s, 0, hi), (True, s, 0, hi)]
    p, m = zp(p[:mid]), zm(m[mid:])
    blocks += [p, m, xp(p), xm(m)]
    places += [(False, 4, 0, mid), (False, 4, mid, hi), (True, 4, 0, mid), (True, 4, mid, hi)]

    w_mine = lax.all_gather(half(second_weight, 0), FS, axis=0, tiled=True)
    w_theirs = swap(w_mine)

    own = mels.reshape(span, stack)
    edge = lax.dynamic_slice_in_dim(own, c * (span - HALF), HALF, axis=0)
    n_tm = 16
    out_pairs = [(2 * j + 1, 2 * j + 2) for j in range(n_tm // 2 - 1)]
    halo = lax.ppermute(edge, TM, out_pairs + [(b, a) for a, b in out_pairs])
    recv = swap(jnp.concatenate([own, halo]))

    rows = 2 * span + 2 * HALF
    ends = jnp.cumsum(utt_lengths.reshape(-1))
    positions = chip * 2 * span - HALF + jnp.arange(rows, dtype=jnp.int32)
    ids = jnp.sum((positions[:, None] >= ends[None, :]).astype(jnp.int32), axis=1)
    meta = jnp.stack([c, z, xl]).astype(jnp.int32)
    taps = half(dw_kernel, 0).astype(jnp.float32).reshape(KW, hw // 128, 128).transpose(1, 0, 2)

    bf, f32 = jnp.bfloat16, jnp.float32
    n_in = 4 + 2 * len(blocks)
    sub, act_own, act_send = pl.pallas_call(
        functools.partial(front_kernel, places),
        out_shape=[
            jax.ShapeDtypeStruct((span, width), bf),
            jax.ShapeDtypeStruct((span, hw), bf),
            jax.ShapeDtypeStruct((span, hw), bf),
        ],
        in_specs=[SM, SM] + [ANY] * (3 + len(blocks)) + [VM] * 4,
        out_specs=[ANY] * 3,
        scratch_shapes=[
            pltpu.VMEM((rows, stack), bf),
            pltpu.VMEM((16 * sr, width), bf),
            pltpu.VMEM((16 * fr, width), bf),
            pltpu.VMEM((rows, width), bf),
            pltpu.VMEM((rows, width), bf),
            pltpu.VMEM((hw // 128, rows, 128), f32),
            pltpu.VMEM((rows, 128), jnp.int32),
            pltpu.VMEM((TILE + KW, 128), f32),
            pltpu.VMEM((2 * span, hw), bf),
            pltpu.SemaphoreType.DMA((n_in,)),
            pltpu.SemaphoreType.DMA((3,)),
        ],
        compiler_params=pltpu.CompilerParams(vmem_limit_bytes=48 << 20),
        cost_estimate=pl.CostEstimate(flops=10_000_000_000, bytes_accessed=12 << 20, transcendentals=0),
        name="front",
    )(meta, ids, own, halo, recv, *blocks, norm_gain.reshape(1, width), taps,
      half(bn_scale.reshape(1, width), 0), ids.reshape(rows, 1))

    act_recv = swap(act_send)
    out = pl.pallas_call(
        back_kernel,
        out_shape=jax.ShapeDtypeStruct((span, width), bf),
        in_specs=[SM] + [ANY] * 5,
        out_specs=ANY,
        scratch_shapes=[
            pltpu.VMEM((span, width), bf),
            pltpu.VMEM((span, width), bf),
            pltpu.VMEM((width, width), bf),
            pltpu.VMEM((span, width), bf),
            pltpu.SemaphoreType.DMA((5,)),
            pltpu.SemaphoreType.DMA((4,)),
        ],
        compiler_params=pltpu.CompilerParams(vmem_limit_bytes=32 << 20),
        cost_estimate=pl.CostEstimate(flops=3_600_000_000, bytes_accessed=12 << 20, transcendentals=0),
        name="back",
    )(meta, sub, act_own, act_recv, w_mine, w_theirs)
    return out.reshape(1, span, width)


def solution(mesh):
    fine = Mesh(mesh.devices.reshape(4, 2, 2, 2, 8), ("y", "xh", "c", "xl", "z"))
    in_specs = (
        P(FS, TM, None),
        P(FS, None),
        P(FS, None),
        P(),
        P(FS, None),
        P(),
        P(),
        P(FS, None),
    )
    return jax.shard_map(
        on_device, mesh=fine, in_specs=in_specs, out_specs=P(FS, TM, None), check_vma=False
    )
```

```python
import functools

import jax
import jax.numpy as jnp
from jax import lax
from jax.experimental import pallas as pl
from jax.experimental.pallas import tpu as pltpu
from jax.sharding import Mesh
from jax.sharding import PartitionSpec as P

KW = 32
HALF = KW // 2
TM = ("y", "xh", "c")
FS = ("xl", "z")
CROSS = [
    ((xh * 2 + c) * 2 + xl, ((x2 // 2) * 2 + c) * 2 + x2 % 2)
    for xh in range(2)
    for c in range(2)
    for xl in range(2)
    for x2 in [(xh * 2 + xl + (1 if c == 0 else 3)) % 4]
]
DIAG = [
    (((xh * 2 + c) * 2 + xl) * 8 + z, (((x2 // 2) * 2 + c) * 2 + x2 % 2) * 8 + (z + d) % 8)
    for xh in range(2)
    for c in range(2)
    for xl in range(2)
    for z in range(8)
    for d in [1 if c == 0 else -1]
    for x2 in [(xh * 2 + xl + d) % 4]
]
TILE = 32
ANY = pl.BlockSpec(memory_space=pl.ANY)
VM = pl.BlockSpec(memory_space=pltpu.VMEM)
SM = pl.BlockSpec(memory_space=pltpu.SMEM)


def cyc(n, s):
    return [(i, (i + s) % n) for i in range(n)]


def front_kernel(places, meta, ids_s, *refs):
    n = places[-1][0] + 1
    own, halo, recv = refs[:3]
    blocks = refs[3 : 3 + n]
    gain, taps, scale, ids_v, sub_out, act_own, act_send = refs[3 + n : 10 + n]
    mels, ws, wf, sub, normed, xs, idb, tmp, act, sem_in, sem_out = refs[10 + n :]
    c, z, xl = meta[0], meta[1], meta[2]
    span = own.shape[0]
    rows = mels.shape[0]
    width = sub.shape[1]
    hw = act.shape[1]
    sr = ws.shape[0] // 16
    fr = wf.shape[0] // 16

    mine = pl.multiple_of(HALF + span * c, HALF)
    other = pl.multiple_of(HALF + span * (1 - c), HALF)
    outer = pl.multiple_of((rows - HALF) * c, HALF)
    inner = pl.multiple_of((rows - HALF) * (1 - c), HALF)
    copies = [
        pltpu.make_async_copy(own, mels.at[pl.ds(mine, span)], sem_in.at[0]),
        pltpu.make_async_copy(recv.at[pl.ds(0, span)], mels.at[pl.ds(other, span)], sem_in.at[1]),
        pltpu.make_async_copy(halo, mels.at[pl.ds(outer, HALF)], sem_in.at[2]),
        pltpu.make_async_copy(recv.at[pl.ds(span, HALF)], mels.at[pl.ds(inner, HALF)], sem_in.at[3]),
    ]
    late = []
    at = 4
    for which, base, flip, shift, lo, hi in places:
        block = blocks[which]
        xx = (1 - xl) if flip else xl
        j = xx * 8 + lax.rem(z + shift + 8, 8)
        if lo < sr:
            copies.append(
                pltpu.make_async_copy(
                    block.at[pl.ds(base, sr)],
                    ws.at[pl.ds(pl.multiple_of(j * sr, sr), sr)],
                    sem_in.at[at],
                )
            )
            at += 1
        a, b = max(lo, sr), hi
        late.append(
            pltpu.make_async_copy(
                block.at[pl.ds(base + a - lo, b - a)],
                wf.at[pl.ds(pl.multiple_of(j * fr + (a - sr), 32), b - a)],
                sem_in.at[at],
            )
        )
        at += 1
    for cp in copies + late:
        cp.start()
    idb[...] = jnp.broadcast_to(ids_v[...], idb.shape)
    for cp in copies:
        cp.wait()

    steps = 8
    chunk = 2 * span // steps
    tail = rows - HALF

    def embed(i):
        r = pl.ds(pl.multiple_of(HALF + i * chunk, HALF), chunk)
        sub[r, :] = jnp.dot(mels[r, :], ws[...], preferred_element_type=jnp.float32).astype(
            jnp.bfloat16
        )

    def norm16(at):
        r = pl.ds(pl.multiple_of(at, HALF), HALF)
        f = sub[r, :].astype(jnp.float32)
        mean = jnp.sum(f, axis=1, keepdims=True) * (1.0 / width)
        d = f - mean
        var = jnp.sum(d * d, axis=1, keepdims=True) * (1.0 / width)
        normed[r, :] = (d * lax.rsqrt(var + 1e-05) * gain[...]).astype(jnp.bfloat16)

    def norm(i):
        for q in range(chunk // HALF):
            norm16(HALF + i * chunk + q * HALF)

    ends = jnp.concatenate([mels[0:HALF, :], mels[tail:, :]])
    s = jnp.dot(ends, ws[...], preferred_element_type=jnp.float32).astype(jnp.bfloat16)
    sub[0:HALF, :] = s[:HALF]
    sub[tail:, :] = s[HALF:]
    embed(0)
    norm16(0)
    norm16(tail)

    def front(i, _):
        embed(i)
        norm(i - 1)
        return 0

    lax.fori_loop(1, steps, front, 0)
    norm(steps - 1)
    out_sub = pltpu.make_async_copy(sub.at[pl.ds(mine, span)], sub_out, sem_out.at[0])
    out_sub.start()
    for cp in late:
        cp.wait()

    def gated(lhs, cg):
        vcol, gcol = cg * 256, hw + cg * 256
        v = jnp.dot(lhs, wf[:, vcol : vcol + 256], preferred_element_type=jnp.float32)
        g = jnp.dot(lhs, wf[:, gcol : gcol + 256], preferred_element_type=jnp.float32)
        return (v * jax.nn.sigmoid(g)).astype(jnp.bfloat16).astype(jnp.float32)

    def edges(cg):
        glu = gated(jnp.concatenate([normed[0:HALF, :], normed[tail:, :]]), cg)
        for h in range(2):
            part = glu[:, h * 128 : (h + 1) * 128]
            xs[2 * cg + h, 0:HALF, :] = part[:HALF]
            xs[2 * cg + h, tail:, :] = part[HALF:]

    def project(i, cg):
        r = pl.ds(pl.multiple_of(HALF + i * chunk, HALF), chunk)
        glu = gated(normed[r, :], cg)
        for h in range(2):
            xs[2 * cg + h, r, :] = glu[:, h * 128 : (h + 1) * 128]

    win = TILE + KW

    def conv(g, t0, u, buf):
        buf[...] = jnp.where(idb[pl.ds(t0, win), :] == u, xs[g, pl.ds(t0, win), :], 0.0)
        s = None
        for b in range(8):
            y = buf[b : b + TILE + KW - 8, :]
            for a in range(KW // 8):
                k = 8 * a + b
                term = y[8 * a : 8 * a + TILE] * taps[g, k : k + 1, :]
                s = term if s is None else s + term
        v = s * scale[:, g * 128 : (g + 1) * 128]
        return (v * jax.nn.sigmoid(v)).astype(jnp.bfloat16)

    def tiles(i, cg):
        for q in range(chunk // TILE):
            t0 = pl.multiple_of(i * chunk + q * TILE, TILE)
            for g in (2 * cg, 2 * cg + 1):
                act[pl.ds(t0, TILE), g * 128 : (g + 1) * 128] = conv(
                    g, t0, ids_s[t0 + HALF], tmp.at[(2 * q + g) % 4]
                )

        def again(q, _):
            t0 = pl.multiple_of(i * chunk + q * TILE, TILE)

            def one(u, _):
                keep = idb[pl.ds(pl.multiple_of(t0 + HALF, HALF), TILE), :] == u
                for g in (2 * cg, 2 * cg + 1):
                    cols = slice(g * 128, (g + 1) * 128)
                    new = conv(g, t0, u, tmp.at[g % 4]).astype(jnp.float32)
                    old = act[pl.ds(t0, TILE), cols].astype(jnp.float32)
                    act[pl.ds(t0, TILE), cols] = jnp.where(keep, new, old).astype(jnp.bfloat16)
                return 0

            lax.fori_loop(ids_s[t0 + HALF] + 1, ids_s[t0 + HALF + TILE - 1] + 1, one, 0)
            return 0

        lax.fori_loop(0, chunk // TILE, again, 0)

    groups = hw // 256
    for cg in range(groups):
        edges(cg)

    def lead(i, _):
        project(i, 0)
        return 0

    lax.fori_loop(0, steps, lead, 0)
    for cg in range(groups):

        def both(i, _):
            if cg + 1 < groups:
                project(i, cg + 1)
            tiles(i, cg)
            return 0

        lax.fori_loop(0, steps, both, 0)

    outs = [
        pltpu.make_async_copy(
            act.at[pl.ds(pl.multiple_of(span * c, span), span)], act_own, sem_out.at[1]
        ),
        pltpu.make_async_copy(
            act.at[pl.ds(pl.multiple_of(span * (1 - c), span), span)], act_send, sem_out.at[2]
        ),
    ]
    for cp in outs:
        cp.start()
    out_sub.wait()
    for cp in outs:
        cp.wait()


def back_kernel(meta, sub, mine, theirs, w, out, sub_v, a_v, w_v, o_v, sem_in, sem_out):
    c = meta[0]
    span, width = sub.shape
    hw = mine.shape[1]
    here = pl.multiple_of(hw * c, 128)
    there = pl.multiple_of(hw * (1 - c), 128)
    copies = [
        pltpu.make_async_copy(
            w.at[j, h],
            w_v.at[pl.ds(j * w.shape[2], w.shape[2]), pl.ds(h * hw, hw)],
            sem_in.at[2 * j + h],
        )
        for j in range(w.shape[0])
        for h in range(2)
    ]
    first = len(copies)
    copies += [
        pltpu.make_async_copy(mine, a_v.at[:, pl.ds(here, hw)], sem_in.at[first]),
        pltpu.make_async_copy(theirs, a_v.at[:, pl.ds(there, hw)], sem_in.at[first + 1]),
        pltpu.make_async_copy(sub, sub_v, sem_in.at[first + 2]),
    ]
    for cp in copies:
        cp.start()
    for cp in copies:
        cp.wait()
    nb = 192
    outs = []
    for i in range(span // nb):
        r = pl.ds(i * nb, nb)
        for n in range(0, width, 512):
            y = jnp.dot(a_v[r, :], w_v[:, n : n + 512], preferred_element_type=jnp.float32)
            o_v[r, n : n + 512] = (sub_v[r, n : n + 512].astype(jnp.float32) + y).astype(
                jnp.bfloat16
            )
        outs.append(pltpu.make_async_copy(o_v.at[r], out.at[r], sem_out.at[i]))
        outs[-1].start()
    for cp in outs:
        cp.wait()


def on_device(mels, utt_lengths, sub_weight, norm_gain, first_weight, dw_kernel, bn_scale, second_weight):
    _, span, stack = mels.shape
    width = second_weight.shape[1]
    hw = width // 2
    sr, fr = sub_weight.shape[0], first_weight.shape[0]
    c = lax.axis_index("c")
    z = lax.axis_index("z")
    xl = lax.axis_index("xl")
    chip = lax.axis_index("y") * 2 + lax.axis_index("xh")
    barrier = lax.optimization_barrier
    zshift = lambda a, s: lax.ppermute(a, "z", cyc(8, s))
    cross = lambda a: lax.ppermute(a, ("xh", "c", "xl"), CROSS)
    swap = lambda a: lax.ppermute(a, "c", cyc(2, 1))

    half = lambda a, at: lax.dynamic_slice_in_dim(a, at + c * hw, hw, axis=a.ndim - 1)
    block = jnp.concatenate(
        [sub_weight, jnp.concatenate([half(first_weight, 0), half(first_weight, width)], axis=1)]
    )
    hi = sr + fr
    mid = hi // 2
    blocks, places = [], []

    def landed(array, parts):
        at = 0
        for flip, shift, lo, up in parts:
            places.append((len(blocks), at, flip, shift, lo, up))
            at += up - lo
        blocks.append(array)

    p = m = block
    crossed = [cross(block)]
    for s in (1, 2, 3):
        p, m = zshift(p, 1), zshift(m, -1)
        if s > 1:
            p, m, crossed[s - 2] = barrier((p, m, crossed[s - 2]))
        landed(p, [(False, -s, 0, hi)])
        landed(m, [(False, s, 0, hi)])
        crossed.append(cross(jnp.concatenate([p, m])))
    landed(block, [(False, 0, 0, hi)])
    for s, array in enumerate(crossed):
        landed(array, [(True, -s, 0, hi), (True, s, 0, hi)] if s else [(True, 0, 0, hi)])
    landed(lax.ppermute(jnp.where(c == 0, p, m), ("xh", "c", "xl", "z"), DIAG), [(True, 4, 0, hi)])
    landed(zshift(p[:mid], 1), [(False, 4, 0, mid)])
    landed(zshift(m[mid:], -1), [(False, 4, mid, hi)])

    w_back = lax.all_gather(half(second_weight, 0), FS + ("c",), axis=0, tiled=True)
    w_back = w_back.reshape(16, 2, fr, hw)

    own = mels.reshape(span, stack)
    edge = lax.dynamic_slice_in_dim(own, c * (span - HALF), HALF, axis=0)
    n_tm = 16
    out_pairs = [(2 * j + 1, 2 * j + 2) for j in range(n_tm // 2 - 1)]
    halo = lax.ppermute(edge, TM, out_pairs + [(b, a) for a, b in out_pairs])
    recv = swap(jnp.concatenate([own, halo]))

    rows = 2 * span + 2 * HALF
    ends = jnp.cumsum(utt_lengths.reshape(-1))
    positions = chip * 2 * span - HALF + jnp.arange(rows, dtype=jnp.int32)
    ids = jnp.sum((positions[:, None] >= ends[None, :]).astype(jnp.int32), axis=1)
    meta = jnp.stack([c, z, xl]).astype(jnp.int32)
    taps = half(dw_kernel, 0).astype(jnp.float32).reshape(KW, hw // 128, 128).transpose(1, 0, 2)

    bf, f32 = jnp.bfloat16, jnp.float32
    n_in = 4 + 2 * len(places)
    sub, act_own, act_send = pl.pallas_call(
        functools.partial(front_kernel, places),
        out_shape=[
            jax.ShapeDtypeStruct((span, width), bf),
            jax.ShapeDtypeStruct((span, hw), bf),
            jax.ShapeDtypeStruct((span, hw), bf),
        ],
        in_specs=[SM, SM] + [ANY] * (3 + len(blocks)) + [VM] * 4,
        out_specs=[ANY] * 3,
        scratch_shapes=[
            pltpu.VMEM((rows, stack), bf),
            pltpu.VMEM((16 * sr, width), bf),
            pltpu.VMEM((16 * fr, width), bf),
            pltpu.VMEM((rows, width), bf),
            pltpu.VMEM((rows, width), bf),
            pltpu.VMEM((hw // 128, rows, 128), f32),
            pltpu.VMEM((rows, 128), jnp.int32),
            pltpu.VMEM((4, TILE + KW, 128), f32),
            pltpu.VMEM((2 * span, hw), bf),
            pltpu.SemaphoreType.DMA((n_in,)),
            pltpu.SemaphoreType.DMA((3,)),
        ],
        compiler_params=pltpu.CompilerParams(vmem_limit_bytes=48 << 20),
        cost_estimate=pl.CostEstimate(flops=10_000_000_000, bytes_accessed=12 << 20, transcendentals=0),
        name="front",
    )(meta, ids, own, halo, recv, *blocks, norm_gain.reshape(1, width), taps,
      half(bn_scale.reshape(1, width), 0), ids.reshape(rows, 1))

    w_back, act_send = barrier((w_back, act_send))
    act_recv = swap(act_send)
    out = pl.pallas_call(
        back_kernel,
        out_shape=jax.ShapeDtypeStruct((span, width), bf),
        in_specs=[SM] + [ANY] * 4,
        out_specs=ANY,
        scratch_shapes=[
            pltpu.VMEM((span, width), bf),
            pltpu.VMEM((span, width), bf),
            pltpu.VMEM((width, width), bf),
            pltpu.VMEM((span, width), bf),
            pltpu.SemaphoreType.DMA((35,)),
            pltpu.SemaphoreType.DMA((4,)),
        ],
        compiler_params=pltpu.CompilerParams(vmem_limit_bytes=60 << 20),
        cost_estimate=pl.CostEstimate(flops=3_600_000_000, bytes_accessed=12 << 20, transcendentals=0),
        name="back",
    )(meta, sub, act_own, act_recv, w_back)
    return out.reshape(1, span, width)


def solution(mesh):
    fine = Mesh(mesh.devices.reshape(4, 2, 2, 2, 8), ("y", "xh", "c", "xl", "z"))
    in_specs = (
        P(FS, TM, None),
        P(FS, None),
        P(FS, None),
        P(),
        P(FS, None),
        P(),
        P(),
        P(FS, None),
    )
    return jax.shard_map(
        on_device, mesh=fine, in_specs=in_specs, out_specs=P(FS, TM, None), check_vma=False
    )
```

```python
import functools

import jax
import jax.numpy as jnp
from jax import lax
from jax.experimental import pallas as pl
from jax.experimental.pallas import tpu as pltpu
from jax.sharding import Mesh
from jax.sharding import PartitionSpec as P

KW = 32
HALF = KW // 2
TM = ("y", "xh", "c")
FS = ("xl", "z")
CROSS = [
    ((xh * 2 + c) * 2 + xl, ((x2 // 2) * 2 + c) * 2 + x2 % 2)
    for xh in range(2)
    for c in range(2)
    for xl in range(2)
    for x2 in [(xh * 2 + xl + (1 if c == 0 else 3)) % 4]
]
DIAG = [
    (((xh * 2 + c) * 2 + xl) * 8 + z, (((x2 // 2) * 2 + c) * 2 + x2 % 2) * 8 + (z + d) % 8)
    for xh in range(2)
    for c in range(2)
    for xl in range(2)
    for z in range(8)
    for d in [1 if c == 0 else -1]
    for x2 in [(xh * 2 + xl + d) % 4]
]
TILE = 32
ANY = pl.BlockSpec(memory_space=pl.ANY)
VM = pl.BlockSpec(memory_space=pltpu.VMEM)
SM = pl.BlockSpec(memory_space=pltpu.SMEM)


def cyc(n, s):
    return [(i, (i + s) % n) for i in range(n)]


def pack_kernel(sub, first, out):
    c = lax.axis_index("c")
    sr, width = sub.shape
    hw = width // 2
    out[0:sr, :] = sub[...]
    for h in range(2):
        cols = pl.ds(pl.multiple_of(h * width + c * hw, 128), hw)
        out[sr:, h * hw : (h + 1) * hw] = first[:, cols]


def front_kernel(places, meta, ids_s, starts, *refs):
    n = places[-1][0] + 1
    own, halo, recv = refs[:3]
    blocks = refs[3 : 3 + n]
    gain, taps, scale, ids_v, sub_out, act_own, act_send = refs[3 + n : 10 + n]
    mels, ws, wf, sub, normed, xs, idb, tmp, act, sem_in, sem_out = refs[10 + n :]
    c, z, xl = meta[0], meta[1], meta[2]
    span = own.shape[0]
    rows = mels.shape[0]
    width = sub.shape[1]
    hw = act.shape[1]
    sr = ws.shape[0] // 16
    fr = wf.shape[0] // 16

    mine = pl.multiple_of(HALF + span * c, HALF)
    other = pl.multiple_of(HALF + span * (1 - c), HALF)
    outer = pl.multiple_of((rows - HALF) * c, HALF)
    inner = pl.multiple_of((rows - HALF) * (1 - c), HALF)
    copies = [
        pltpu.make_async_copy(own, mels.at[pl.ds(mine, span)], sem_in.at[0]),
        pltpu.make_async_copy(recv.at[pl.ds(0, span)], mels.at[pl.ds(other, span)], sem_in.at[1]),
        pltpu.make_async_copy(halo, mels.at[pl.ds(outer, HALF)], sem_in.at[2]),
        pltpu.make_async_copy(recv.at[pl.ds(span, HALF)], mels.at[pl.ds(inner, HALF)], sem_in.at[3]),
    ]
    late = []
    at = 4
    for which, base, flip, shift, lo, hi in places:
        block = blocks[which]
        xx = (1 - xl) if flip else xl
        j = xx * 8 + lax.rem(z + shift + 8, 8)
        if lo < sr:
            copies.append(
                pltpu.make_async_copy(
                    block.at[pl.ds(base, sr)],
                    ws.at[pl.ds(pl.multiple_of(j * sr, sr), sr)],
                    sem_in.at[at],
                )
            )
            at += 1
        a, b = max(lo, sr), hi
        late.append(
            pltpu.make_async_copy(
                block.at[pl.ds(base + a - lo, b - a)],
                wf.at[pl.ds(pl.multiple_of(j * fr + (a - sr), 32), b - a)],
                sem_in.at[at],
            )
        )
        at += 1
    for cp in copies + late:
        cp.start()
    idb[...] = jnp.broadcast_to(ids_v[...], idb.shape)
    for cp in copies:
        cp.wait()

    steps = 8
    chunk = 2 * span // steps
    tail = rows - HALF

    def embed(i):
        r = pl.ds(pl.multiple_of(HALF + i * chunk, HALF), chunk)
        sub[r, :] = jnp.dot(mels[r, :], ws[...], preferred_element_type=jnp.float32).astype(
            jnp.bfloat16
        )

    def norm16(at):
        r = pl.ds(pl.multiple_of(at, HALF), HALF)
        f = sub[r, :].astype(jnp.float32)
        mean = jnp.sum(f, axis=1, keepdims=True) * (1.0 / width)
        d = f - mean
        var = jnp.sum(d * d, axis=1, keepdims=True) * (1.0 / width)
        normed[r, :] = (d * lax.rsqrt(var + 1e-05) * gain[...]).astype(jnp.bfloat16)

    def norm(i):
        for q in range(chunk // HALF):
            norm16(HALF + i * chunk + q * HALF)

    ends = jnp.concatenate([mels[0:HALF, :], mels[tail:, :]])
    s = jnp.dot(ends, ws[...], preferred_element_type=jnp.float32).astype(jnp.bfloat16)
    sub[0:HALF, :] = s[:HALF]
    sub[tail:, :] = s[HALF:]
    embed(0)
    norm16(0)
    norm16(tail)

    def front(i, _):
        embed(i)
        norm(i - 1)
        return 0

    lax.fori_loop(1, steps, front, 0)
    norm(steps - 1)
    out_sub = pltpu.make_async_copy(sub.at[pl.ds(mine, span)], sub_out, sem_out.at[0])
    out_sub.start()
    for cp in late:
        cp.wait()

    def gated(lhs, cg):
        vcol, gcol = cg * 256, hw + cg * 256
        v = jnp.dot(lhs, wf[:, vcol : vcol + 256], preferred_element_type=jnp.float32)
        g = jnp.dot(lhs, wf[:, gcol : gcol + 256], preferred_element_type=jnp.float32)
        return (v * jax.nn.sigmoid(g)).astype(jnp.bfloat16).astype(jnp.float32)

    def edges(cg):
        glu = gated(jnp.concatenate([normed[0:HALF, :], normed[tail:, :]]), cg)
        for h in range(2):
            part = glu[:, h * 128 : (h + 1) * 128]
            xs[2 * cg + h, 0:HALF, :] = part[:HALF]
            xs[2 * cg + h, tail:, :] = part[HALF:]

    def project(i, cg):
        r = pl.ds(pl.multiple_of(HALF + i * chunk, HALF), chunk)
        glu = gated(normed[r, :], cg)
        for h in range(2):
            xs[2 * cg + h, r, :] = glu[:, h * 128 : (h + 1) * 128]

    win = TILE + KW

    def conv(g, t0, u, buf):
        buf[...] = jnp.where(idb[pl.ds(t0, win), :] == u, xs[g, pl.ds(t0, win), :], 0.0)
        s = None
        for b in range(8):
            y = buf[b : b + TILE + KW - 8, :]
            for a in range(KW // 8):
                k = 8 * a + b
                term = y[8 * a : 8 * a + TILE].reshape(TILE // 8, 8, 128) * taps[g, k][None]
                s = term if s is None else s + term
        v = s.reshape(TILE, 128) * scale[:, g * 128 : (g + 1) * 128]
        return (v * jax.nn.sigmoid(v)).astype(jnp.bfloat16)

    def tiles(i, cg):
        for q in range(chunk // TILE):
            t0 = pl.multiple_of(i * chunk + q * TILE, TILE)
            for g in (2 * cg, 2 * cg + 1):
                act[pl.ds(t0, TILE), g * 128 : (g + 1) * 128] = conv(
                    g, t0, ids_s[t0 + HALF], tmp.at[(2 * q + g) % 4]
                )

        def again(u, _):
            t0 = pl.multiple_of(jnp.bitwise_and(starts[u], -TILE), TILE)
            keep = idb[pl.ds(pl.multiple_of(t0 + HALF, HALF), TILE), :] == u
            for g in (2 * cg, 2 * cg + 1):
                cols = slice(g * 128, (g + 1) * 128)
                new = conv(g, t0, u, tmp.at[g % 4]).astype(jnp.float32)
                old = act[pl.ds(t0, TILE), cols].astype(jnp.float32)
                act[pl.ds(t0, TILE), cols] = jnp.where(keep, new, old).astype(jnp.bfloat16)
            return 0

        row = i * chunk + HALF
        lax.fori_loop(ids_s[row] + 1, ids_s[row + chunk - 1] + 1, again, 0)

    groups = hw // 256
    for cg in range(groups):
        edges(cg)

    def lead(i, _):
        project(i, 0)
        return 0

    lax.fori_loop(0, steps, lead, 0)
    for cg in range(groups):

        def both(i, _):
            if cg + 1 < groups:
                project(i, cg + 1)
            tiles(i, cg)
            return 0

        lax.fori_loop(0, steps, both, 0)

    outs = [
        pltpu.make_async_copy(
            act.at[pl.ds(pl.multiple_of(span * c, span), span)], act_own, sem_out.at[1]
        ),
        pltpu.make_async_copy(
            act.at[pl.ds(pl.multiple_of(span * (1 - c), span), span)], act_send, sem_out.at[2]
        ),
    ]
    for cp in outs:
        cp.start()
    out_sub.wait()
    for cp in outs:
        cp.wait()


def back_kernel(meta, sub, mine, theirs, w, out, sub_v, a_v, w_v, o_v, sem_in, sem_out):
    c = meta[0]
    span, width = sub.shape
    hw = mine.shape[1]
    here = pl.multiple_of(hw * c, 128)
    there = pl.multiple_of(hw * (1 - c), 128)
    copies = [
        pltpu.make_async_copy(
            w.at[j, h],
            w_v.at[pl.ds(j * w.shape[2], w.shape[2]), pl.ds(h * hw, hw)],
            sem_in.at[2 * j + h],
        )
        for j in range(w.shape[0])
        for h in range(2)
    ]
    first = len(copies)
    copies += [
        pltpu.make_async_copy(mine, a_v.at[:, pl.ds(here, hw)], sem_in.at[first]),
        pltpu.make_async_copy(theirs, a_v.at[:, pl.ds(there, hw)], sem_in.at[first + 1]),
        pltpu.make_async_copy(sub, sub_v, sem_in.at[first + 2]),
    ]
    order = [cp for cp in copies[first:]] + [cp for h in range(2) for cp in copies[h:first:2]]
    for cp in order:
        cp.start()
    for cp in copies[first:]:
        cp.wait()
    nb = 256
    outs = []
    for h in range(2):
        for cp in copies[h:first:2]:
            cp.wait()
        for i in range(span // nb):
            r = pl.ds(i * nb, nb)
            for n in range(h * hw, (h + 1) * hw, 256):
                y = jnp.dot(a_v[r, :], w_v[:, n : n + 256], preferred_element_type=jnp.float32)
                o_v[r, n : n + 256] = (sub_v[r, n : n + 256].astype(jnp.float32) + y).astype(
                    jnp.bfloat16
                )
            cols = pl.ds(h * hw, hw)
            outs.append(pltpu.make_async_copy(o_v.at[r, cols], out.at[r, cols], sem_out.at[len(outs)]))
            outs[-1].start()
    for cp in outs:
        cp.wait()


def on_device(mels, utt_lengths, sub_weight, norm_gain, first_weight, dw_kernel, bn_scale, second_weight):
    _, span, stack = mels.shape
    width = second_weight.shape[1]
    hw = width // 2
    sr, fr = sub_weight.shape[0], first_weight.shape[0]
    c = lax.axis_index("c")
    z = lax.axis_index("z")
    xl = lax.axis_index("xl")
    chip = lax.axis_index("y") * 2 + lax.axis_index("xh")
    barrier = lax.optimization_barrier
    zshift = lambda a, s: lax.ppermute(a, "z", cyc(8, s))
    cross = lambda a: lax.ppermute(a, ("xh", "c", "xl"), CROSS)
    swap = lambda a: lax.ppermute(a, "c", cyc(2, 1))

    half = lambda a, at: lax.dynamic_slice_in_dim(a, at + c * hw, hw, axis=a.ndim - 1)
    hi = sr + fr
    block = pl.pallas_call(
        pack_kernel,
        out_shape=jax.ShapeDtypeStruct((hi, width), jnp.bfloat16),
        in_specs=[VM] * 2,
        out_specs=VM,
        name="front_pack",
    )(sub_weight, first_weight)
    rows = 2 * span + 2 * HALF
    ends = jnp.cumsum(utt_lengths.reshape(-1))
    positions = chip * 2 * span - HALF + jnp.arange(rows, dtype=jnp.int32)
    ids = jnp.sum((positions[:, None] >= ends[None, :]).astype(jnp.int32), axis=1)
    meta = jnp.stack([c, z, xl]).astype(jnp.int32)
    starts = jnp.concatenate([jnp.zeros(1, jnp.int32), ends]) - chip * 2 * span
    taps = half(dw_kernel, 0).astype(jnp.float32).reshape(KW, hw // 128, 128).transpose(1, 0, 2)
    taps = jnp.broadcast_to(taps[:, :, None, :], (hw // 128, KW, 8, 128))
    gain = norm_gain.reshape(1, width)
    scale = half(bn_scale.reshape(1, width), 0)
    small = (meta, ids, ids.reshape(rows, 1), starts, taps, gain, scale)

    blocks, places = [], []

    own = mels.reshape(span, stack)
    edge = lax.dynamic_slice_in_dim(own, c * (span - HALF), HALF, axis=0)
    n_tm = 16
    out_pairs = [(2 * j + 1, 2 * j + 2) for j in range(n_tm // 2 - 1)]
    halo = lax.ppermute(edge, TM, out_pairs + [(b, a) for a, b in out_pairs])

    def landed(array, parts):
        at = 0
        for flip, shift, lo, up in parts:
            places.append((len(blocks), at, flip, shift, lo, up))
            at += up - lo
        blocks.append(array)

    w_half = half(second_weight, 0)
    p = m = block
    crossed = [cross(block)]
    for s in (1, 2, 3):
        p, m = zshift(p, 1), zshift(m, -1)
        if s == 1:
            p, m, small = barrier((p, m, small))
        elif s == 2:
            p, m, crossed[0] = barrier((p, m, crossed[0]))
        elif s == 3:
            p, m, crossed[1] = barrier((p, m, crossed[1]))
        landed(p, [(False, -s, 0, hi)])
        landed(m, [(False, s, 0, hi)])
        crossed.append(cross(jnp.concatenate([p, m])))
    landed(block, [(False, 0, 0, hi)])
    for s, array in enumerate(crossed):
        landed(array, [(True, -s, 0, hi), (True, s, 0, hi)] if s else [(True, 0, 0, hi)])
    landed(lax.ppermute(jnp.where(c == 0, p, m), ("xh", "c", "xl", "z"), DIAG), [(True, 4, 0, hi)])
    landed(zshift(p[: hi // 2], 1), [(False, 4, 0, hi // 2)])
    landed(zshift(m[hi // 2 :], -1), [(False, 4, hi // 2, hi)])

    recv = swap(jnp.concatenate([own, halo]))
    w_back = lax.all_gather(w_half, FS + ("c",), axis=0, tiled=True)
    w_back = w_back.reshape(16, 2, fr, hw)

    meta, ids, ids_col, starts, taps, gain, scale = small
    bf, f32 = jnp.bfloat16, jnp.float32
    n_in = 4 + 2 * len(places)
    sub, act_own, act_send = pl.pallas_call(
        functools.partial(front_kernel, places),
        out_shape=[
            jax.ShapeDtypeStruct((span, width), bf),
            jax.ShapeDtypeStruct((span, hw), bf),
            jax.ShapeDtypeStruct((span, hw), bf),
        ],
        in_specs=[SM] * 3 + [ANY] * (3 + len(blocks)) + [VM] * 4,
        out_specs=[ANY] * 3,
        scratch_shapes=[
            pltpu.VMEM((rows, stack), bf),
            pltpu.VMEM((16 * sr, width), bf),
            pltpu.VMEM((16 * fr, width), bf),
            pltpu.VMEM((rows, width), bf),
            pltpu.VMEM((rows, width), bf),
            pltpu.VMEM((hw // 128, rows, 128), f32),
            pltpu.VMEM((rows, 128), jnp.int32),
            pltpu.VMEM((4, TILE + KW, 128), f32),
            pltpu.VMEM((2 * span, hw), bf),
            pltpu.SemaphoreType.DMA((n_in,)),
            pltpu.SemaphoreType.DMA((3,)),
        ],
        compiler_params=pltpu.CompilerParams(vmem_limit_bytes=48 << 20),
        cost_estimate=pl.CostEstimate(flops=10_000_000_000, bytes_accessed=12 << 20, transcendentals=0),
        name="front",
    )(meta, ids, starts, own, halo, recv, *blocks, gain, taps, scale, ids_col)

    w_back, act_send = barrier((w_back, act_send))
    act_recv = swap(act_send)
    out = pl.pallas_call(
        back_kernel,
        out_shape=jax.ShapeDtypeStruct((span, width), bf),
        in_specs=[SM] + [ANY] * 4,
        out_specs=ANY,
        scratch_shapes=[
            pltpu.VMEM((span, width), bf),
            pltpu.VMEM((span, width), bf),
            pltpu.VMEM((width, width), bf),
            pltpu.VMEM((span, width), bf),
            pltpu.SemaphoreType.DMA((35,)),
            pltpu.SemaphoreType.DMA((6,)),
        ],
        compiler_params=pltpu.CompilerParams(vmem_limit_bytes=60 << 20),
        cost_estimate=pl.CostEstimate(flops=3_600_000_000, bytes_accessed=12 << 20, transcendentals=0),
        name="back",
    )(meta, sub, act_own, act_recv, w_back)
    return out.reshape(1, span, width)


def solution(mesh):
    fine = Mesh(mesh.devices.reshape(4, 2, 2, 2, 8), ("y", "xh", "c", "xl", "z"))
    in_specs = (
        P(FS, TM, None),
        P(FS, None),
        P(FS, None),
        P(),
        P(FS, None),
        P(),
        P(),
        P(FS, None),
    )
    return jax.shard_map(
        on_device, mesh=fine, in_specs=in_specs, out_specs=P(FS, TM, None), check_vma=False
    )
```

```python
import functools

import jax
import jax.numpy as jnp
from jax import lax
from jax.experimental import pallas as pl
from jax.experimental.pallas import tpu as pltpu
from jax.sharding import Mesh
from jax.sharding import PartitionSpec as P

KW = 32
HALF = KW // 2
TM = ("y", "xh", "c")
FS = ("xl", "z")
CROSS = [
    ((xh * 2 + c) * 2 + xl, ((x2 // 2) * 2 + c) * 2 + x2 % 2)
    for xh in range(2)
    for c in range(2)
    for xl in range(2)
    for x2 in [(xh * 2 + xl + (1 if c == 0 else 3)) % 4]
]
DIAG = [
    (((xh * 2 + c) * 2 + xl) * 8 + z, (((x2 // 2) * 2 + c) * 2 + x2 % 2) * 8 + (z + d) % 8)
    for xh in range(2)
    for c in range(2)
    for xl in range(2)
    for z in range(8)
    for d in [1 if c == 0 else -1]
    for x2 in [(xh * 2 + xl + d) % 4]
]
TILE = 32
ANY = pl.BlockSpec(memory_space=pl.ANY)
VM = pl.BlockSpec(memory_space=pltpu.VMEM)
SM = pl.BlockSpec(memory_space=pltpu.SMEM)


def cyc(n, s):
    return [(i, (i + s) % n) for i in range(n)]


def pack_kernel(sub, first, out):
    c = lax.axis_index("c")
    sr, width = sub.shape
    hw = width // 2
    out[0:sr, :] = sub[...]
    for h in range(2):
        cols = pl.ds(pl.multiple_of(h * width + c * hw, 128), hw)
        out[sr:, h * hw : (h + 1) * hw] = first[:, cols]


def front_kernel(places, meta, ids_s, starts, *refs):
    n = places[-1][0] + 1
    own, halo, recv = refs[:3]
    blocks = refs[3 : 3 + n]
    gain, taps, scale, ids_v, sub_out, act_own, act_send = refs[3 + n : 10 + n]
    mels, ws, wf, sub, normed, xs, idb, tmp, act, sem_in, sem_out = refs[10 + n :]
    c, z, xl = meta[0], meta[1], meta[2]
    span = own.shape[0]
    rows = mels.shape[0]
    width = sub.shape[1]
    hw = act.shape[1]
    sr = ws.shape[0] // 16
    fr = wf.shape[0] // 16

    mine = pl.multiple_of(HALF + span * c, HALF)
    other = pl.multiple_of(HALF + span * (1 - c), HALF)
    outer = pl.multiple_of((rows - HALF) * c, HALF)
    inner = pl.multiple_of((rows - HALF) * (1 - c), HALF)
    copies = [
        pltpu.make_async_copy(own, mels.at[pl.ds(mine, span)], sem_in.at[0]),
        pltpu.make_async_copy(recv.at[pl.ds(0, span)], mels.at[pl.ds(other, span)], sem_in.at[1]),
        pltpu.make_async_copy(halo, mels.at[pl.ds(outer, HALF)], sem_in.at[2]),
        pltpu.make_async_copy(recv.at[pl.ds(span, HALF)], mels.at[pl.ds(inner, HALF)], sem_in.at[3]),
    ]
    late = []
    at = 4
    for which, base, flip, shift, lo, hi in places:
        block = blocks[which]
        xx = (1 - xl) if flip else xl
        j = xx * 8 + lax.rem(z + shift + 8, 8)
        if lo < sr:
            copies.append(
                pltpu.make_async_copy(
                    block.at[pl.ds(base, sr)],
                    ws.at[pl.ds(pl.multiple_of(j * sr, sr), sr)],
                    sem_in.at[at],
                )
            )
            at += 1
        a, b = max(lo, sr), hi
        late.append(
            pltpu.make_async_copy(
                block.at[pl.ds(base + a - lo, b - a)],
                wf.at[pl.ds(pl.multiple_of(j * fr + (a - sr), 32), b - a)],
                sem_in.at[at],
            )
        )
        at += 1
    for cp in copies + late:
        cp.start()
    idb[...] = jnp.broadcast_to(ids_v[...], idb.shape)
    for cp in copies:
        cp.wait()

    steps = 8
    chunk = 2 * span // steps
    tail = rows - HALF

    def embed(i):
        r = pl.ds(pl.multiple_of(HALF + i * chunk, HALF), chunk)
        sub[r, :] = jnp.dot(mels[r, :], ws[...], preferred_element_type=jnp.float32).astype(
            jnp.bfloat16
        )

    def norm16(at):
        r = pl.ds(pl.multiple_of(at, HALF), HALF)
        f = sub[r, :].astype(jnp.float32)
        mean = jnp.sum(f, axis=1, keepdims=True) * (1.0 / width)
        d = f - mean
        var = jnp.sum(d * d, axis=1, keepdims=True) * (1.0 / width)
        normed[r, :] = (d * lax.rsqrt(var + 1e-05) * gain[...]).astype(jnp.bfloat16)

    def norm(i):
        for q in range(chunk // HALF):
            norm16(HALF + i * chunk + q * HALF)

    ends = jnp.concatenate([mels[0:HALF, :], mels[tail:, :]])
    s = jnp.dot(ends, ws[...], preferred_element_type=jnp.float32).astype(jnp.bfloat16)
    sub[0:HALF, :] = s[:HALF]
    sub[tail:, :] = s[HALF:]
    embed(0)
    norm16(0)
    norm16(tail)

    def front(i, _):
        embed(i)
        norm(i - 1)
        return 0

    lax.fori_loop(1, steps, front, 0)
    norm(steps - 1)
    out_sub = pltpu.make_async_copy(sub.at[pl.ds(mine, span)], sub_out, sem_out.at[0])
    out_sub.start()
    for cp in late:
        cp.wait()

    def gated(lhs, cg):
        vcol, gcol = cg * 256, hw + cg * 256
        v = jnp.dot(lhs, wf[:, vcol : vcol + 256], preferred_element_type=jnp.float32)
        g = jnp.dot(lhs, wf[:, gcol : gcol + 256], preferred_element_type=jnp.float32)
        return (v * jax.nn.sigmoid(g)).astype(jnp.bfloat16).astype(jnp.float32)

    def edges(cg):
        glu = gated(jnp.concatenate([normed[0:HALF, :], normed[tail:, :]]), cg)
        for h in range(2):
            part = glu[:, h * 128 : (h + 1) * 128]
            xs[2 * cg + h, 0:HALF, :] = part[:HALF]
            xs[2 * cg + h, tail:, :] = part[HALF:]

    def project(i, cg):
        r = pl.ds(pl.multiple_of(HALF + i * chunk, HALF), chunk)
        glu = gated(normed[r, :], cg)
        for h in range(2):
            xs[2 * cg + h, r, :] = glu[:, h * 128 : (h + 1) * 128]

    win = TILE + KW

    def conv(g, t0, u, buf):
        buf[...] = jnp.where(idb[pl.ds(t0, win), :] == u, xs[g, pl.ds(t0, win), :], 0.0)
        s = None
        for b in range(8):
            y = buf[b : b + TILE + KW - 8, :]
            for a in range(KW // 8):
                k = 8 * a + b
                term = y[8 * a : 8 * a + TILE].reshape(TILE // 8, 8, 128) * taps[g, k][None]
                s = term if s is None else s + term
        v = s.reshape(TILE, 128) * scale[:, g * 128 : (g + 1) * 128]
        return (v * jax.nn.sigmoid(v)).astype(jnp.bfloat16)

    def tiles(i, cg):
        for q in range(chunk // TILE):
            t0 = pl.multiple_of(i * chunk + q * TILE, TILE)
            for g in (2 * cg, 2 * cg + 1):
                act[pl.ds(t0, TILE), g * 128 : (g + 1) * 128] = conv(
                    g, t0, ids_s[t0 + HALF], tmp.at[(2 * q + g) % 4]
                )

        def again(u, _):
            t0 = pl.multiple_of(jnp.bitwise_and(starts[u], -TILE), TILE)
            keep = idb[pl.ds(pl.multiple_of(t0 + HALF, HALF), TILE), :] == u
            for g in (2 * cg, 2 * cg + 1):
                cols = slice(g * 128, (g + 1) * 128)
                new = conv(g, t0, u, tmp.at[g % 4]).astype(jnp.float32)
                old = act[pl.ds(t0, TILE), cols].astype(jnp.float32)
                act[pl.ds(t0, TILE), cols] = jnp.where(keep, new, old).astype(jnp.bfloat16)
            return 0

        row = i * chunk + HALF
        lax.fori_loop(ids_s[row] + 1, ids_s[row + chunk - 1] + 1, again, 0)

    groups = hw // 256
    for cg in range(groups):
        edges(cg)

    def lead(i, _):
        project(i, 0)
        return 0

    lax.fori_loop(0, steps, lead, 0)
    for cg in range(groups):

        def both(i, _):
            if cg + 1 < groups:
                project(i, cg + 1)
            tiles(i, cg)
            return 0

        lax.fori_loop(0, steps, both, 0)

    outs = [
        pltpu.make_async_copy(
            act.at[pl.ds(pl.multiple_of(span * c, span), span)], act_own, sem_out.at[1]
        ),
        pltpu.make_async_copy(
            act.at[pl.ds(pl.multiple_of(span * (1 - c), span), span)], act_send, sem_out.at[2]
        ),
    ]
    for cp in outs:
        cp.start()
    out_sub.wait()
    for cp in outs:
        cp.wait()


def back_kernel(meta, sub, mine, theirs, w, out, sub_v, a_v, w_v, o_v, sem_in, sem_out):
    c = meta[0]
    span, width = sub.shape
    hw = mine.shape[1]
    here = pl.multiple_of(hw * c, 128)
    there = pl.multiple_of(hw * (1 - c), 128)
    copies = [
        pltpu.make_async_copy(
            w.at[j, h],
            w_v.at[pl.ds(j * w.shape[2], w.shape[2]), pl.ds(h * hw, hw)],
            sem_in.at[2 * j + h],
        )
        for j in range(w.shape[0])
        for h in range(2)
    ]
    first = len(copies)
    copies += [
        pltpu.make_async_copy(mine, a_v.at[:, pl.ds(here, hw)], sem_in.at[first]),
        pltpu.make_async_copy(theirs, a_v.at[:, pl.ds(there, hw)], sem_in.at[first + 1]),
        pltpu.make_async_copy(sub, sub_v, sem_in.at[first + 2]),
    ]
    order = [cp for cp in copies[first:]] + [cp for h in range(2) for cp in copies[h:first:2]]
    for cp in order:
        cp.start()
    for cp in copies[first:]:
        cp.wait()
    nb = 256
    outs = []
    for h in range(2):
        for cp in copies[h:first:2]:
            cp.wait()
        for i in range(span // nb):
            r = pl.ds(i * nb, nb)
            for n in range(h * hw, (h + 1) * hw, 256):
                y = jnp.dot(a_v[r, :], w_v[:, n : n + 256], preferred_element_type=jnp.float32)
                o_v[r, n : n + 256] = (sub_v[r, n : n + 256].astype(jnp.float32) + y).astype(
                    jnp.bfloat16
                )
            cols = pl.ds(h * hw, hw)
            outs.append(pltpu.make_async_copy(o_v.at[r, cols], out.at[r, cols], sem_out.at[len(outs)]))
            outs[-1].start()
    for cp in outs:
        cp.wait()


def on_device(mels, utt_lengths, sub_weight, norm_gain, first_weight, dw_kernel, bn_scale, second_weight):
    _, span, stack = mels.shape
    width = second_weight.shape[1]
    hw = width // 2
    sr, fr = sub_weight.shape[0], first_weight.shape[0]
    c = lax.axis_index("c")
    z = lax.axis_index("z")
    xl = lax.axis_index("xl")
    chip = lax.axis_index("y") * 2 + lax.axis_index("xh")
    barrier = lax.optimization_barrier
    zshift = lambda a, s: lax.ppermute(a, "z", cyc(8, s))
    cross = lambda a: lax.ppermute(a, ("xh", "c", "xl"), CROSS)
    swap = lambda a: lax.ppermute(a, "c", cyc(2, 1))

    half = lambda a, at: lax.dynamic_slice_in_dim(a, at + c * hw, hw, axis=a.ndim - 1)
    hi = sr + fr
    block = pl.pallas_call(
        pack_kernel,
        out_shape=jax.ShapeDtypeStruct((hi, width), jnp.bfloat16),
        in_specs=[VM] * 2,
        out_specs=VM,
        name="front_pack",
    )(sub_weight, first_weight)
    rows = 2 * span + 2 * HALF
    ends = jnp.cumsum(utt_lengths.reshape(-1))
    positions = chip * 2 * span - HALF + jnp.arange(rows, dtype=jnp.int32)
    ids = jnp.sum((positions[:, None] >= ends[None, :]).astype(jnp.int32), axis=1)
    meta = jnp.stack([c, z, xl]).astype(jnp.int32)
    starts = jnp.concatenate([jnp.zeros(1, jnp.int32), ends]) - chip * 2 * span
    taps = half(dw_kernel, 0).astype(jnp.float32).reshape(KW, hw // 128, 128).transpose(1, 0, 2)
    taps = jnp.broadcast_to(taps[:, :, None, :], (hw // 128, KW, 8, 128))
    gain = norm_gain.reshape(1, width)
    scale = half(bn_scale.reshape(1, width), 0)
    small = (meta, ids, ids.reshape(rows, 1), starts, taps, gain, scale)

    blocks, places = [], []

    own = mels.reshape(span, stack)
    edge = lax.dynamic_slice_in_dim(own, c * (span - HALF), HALF, axis=0)
    n_tm = 16
    out_pairs = [(2 * j + 1, 2 * j + 2) for j in range(n_tm // 2 - 1)]
    halo = lax.ppermute(edge, TM, out_pairs + [(b, a) for a, b in out_pairs])

    def landed(array, parts):
        at = 0
        for flip, shift, lo, up in parts:
            places.append((len(blocks), at, flip, shift, lo, up))
            at += up - lo
        blocks.append(array)

    w_half = half(second_weight, 0)
    p = m = block
    crossed = [cross(block)]
    for s in (1, 2, 3):
        p, m = zshift(p, 1), zshift(m, -1)
        if s == 1:
            p, m, small = barrier((p, m, small))
        elif s == 2:
            p, m, crossed[0] = barrier((p, m, crossed[0]))
        elif s == 3:
            p, m, crossed[1] = barrier((p, m, crossed[1]))
        landed(p, [(False, -s, 0, hi)])
        landed(m, [(False, s, 0, hi)])
        crossed.append(cross(jnp.concatenate([p, m])))
    landed(block, [(False, 0, 0, hi)])
    for s, array in enumerate(crossed):
        landed(array, [(True, -s, 0, hi), (True, s, 0, hi)] if s else [(True, 0, 0, hi)])
    landed(lax.ppermute(jnp.where(c == 0, p, m), ("xh", "c", "xl", "z"), DIAG), [(True, 4, 0, hi)])
    landed(zshift(p[: hi // 2], 1), [(False, 4, 0, hi // 2)])
    landed(zshift(m[hi // 2 :], -1), [(False, 4, hi // 2, hi)])

    recv = swap(jnp.concatenate([own, halo]))
    w_back = lax.all_gather(w_half, FS + ("c",), axis=0, tiled=True)
    w_back = w_back.reshape(16, 2, fr, hw)

    meta, ids, ids_col, starts, taps, gain, scale = small
    bf, f32 = jnp.bfloat16, jnp.float32
    n_in = 4 + 2 * len(places)
    sub, act_own, act_send = pl.pallas_call(
        functools.partial(front_kernel, places),
        out_shape=[
            jax.ShapeDtypeStruct((span, width), bf),
            jax.ShapeDtypeStruct((span, hw), bf),
            jax.ShapeDtypeStruct((span, hw), bf),
        ],
        in_specs=[SM] * 3 + [ANY] * (3 + len(blocks)) + [VM] * 4,
        out_specs=[ANY] * 3,
        scratch_shapes=[
            pltpu.VMEM((rows, stack), bf),
            pltpu.VMEM((16 * sr, width), bf),
            pltpu.VMEM((16 * fr, width), bf),
            pltpu.VMEM((rows, width), bf),
            pltpu.VMEM((rows, width), bf),
            pltpu.VMEM((hw // 128, rows, 128), f32),
            pltpu.VMEM((rows, 128), jnp.int32),
            pltpu.VMEM((4, TILE + KW, 128), f32),
            pltpu.VMEM((2 * span, hw), bf),
            pltpu.SemaphoreType.DMA((n_in,)),
            pltpu.SemaphoreType.DMA((3,)),
        ],
        compiler_params=pltpu.CompilerParams(vmem_limit_bytes=60 << 20),
        cost_estimate=pl.CostEstimate(flops=10_000_000_000, bytes_accessed=12 << 20, transcendentals=0),
        name="front",
    )(meta, ids, starts, own, halo, recv, *blocks, gain, taps, scale, ids_col)

    w_back, act_send = barrier((w_back, act_send))
    act_recv = swap(act_send)
    out = pl.pallas_call(
        back_kernel,
        out_shape=jax.ShapeDtypeStruct((span, width), bf),
        in_specs=[SM] + [ANY] * 2 + [VM] + [ANY],
        out_specs=ANY,
        scratch_shapes=[
            pltpu.VMEM((span, width), bf),
            pltpu.VMEM((span, width), bf),
            pltpu.VMEM((width, width), bf),
            pltpu.VMEM((span, width), bf),
            pltpu.SemaphoreType.DMA((35,)),
            pltpu.SemaphoreType.DMA((6,)),
        ],
        compiler_params=pltpu.CompilerParams(vmem_limit_bytes=60 << 20),
        cost_estimate=pl.CostEstimate(flops=3_600_000_000, bytes_accessed=12 << 20, transcendentals=0),
        name="back",
    )(meta, sub, act_own, act_recv, w_back)
    return out.reshape(1, span, width)


def solution(mesh):
    fine = Mesh(mesh.devices.reshape(4, 2, 2, 2, 8), ("y", "xh", "c", "xl", "z"))
    in_specs = (
        P(FS, TM, None),
        P(FS, None),
        P(FS, None),
        P(),
        P(FS, None),
        P(),
        P(),
        P(FS, None),
    )
    return jax.shard_map(
        on_device, mesh=fine, in_specs=in_specs, out_specs=P(FS, TM, None), check_vma=False
    )
```

```python
import functools

import jax
import jax.numpy as jnp
from jax import lax
from jax.experimental import pallas as pl
from jax.experimental.pallas import tpu as pltpu
from jax.sharding import Mesh
from jax.sharding import PartitionSpec as P

KW = 32
HALF = KW // 2
TM = ("y", "xh", "c")
FS = ("xl", "z")
CROSS = [
    ((xh * 2 + c) * 2 + xl, ((x2 // 2) * 2 + c) * 2 + x2 % 2)
    for xh in range(2)
    for c in range(2)
    for xl in range(2)
    for x2 in [(xh * 2 + xl + (1 if c == 0 else 3)) % 4]
]
DIAG = [
    (((xh * 2 + c) * 2 + xl) * 8 + z, (((x2 // 2) * 2 + c) * 2 + x2 % 2) * 8 + (z + d) % 8)
    for xh in range(2)
    for c in range(2)
    for xl in range(2)
    for z in range(8)
    for d in [1 if c == 0 else -1]
    for x2 in [(xh * 2 + xl + d) % 4]
]
TILE = 32
ANY = pl.BlockSpec(memory_space=pl.ANY)
VM = pl.BlockSpec(memory_space=pltpu.VMEM)
SM = pl.BlockSpec(memory_space=pltpu.SMEM)


def cyc(n, s):
    return [(i, (i + s) % n) for i in range(n)]


def pack_kernel(sub, first, out):
    c = lax.axis_index("c")
    sr, width = sub.shape
    hw = width // 2
    out[0:sr, :] = sub[...]
    for h in range(2):
        cols = pl.ds(pl.multiple_of(h * width + c * hw, 128), hw)
        out[sr:, h * hw : (h + 1) * hw] = first[:, cols]


def front_kernel(places, meta, ids_s, starts, *refs):
    n = places[-1][0] + 1
    own, halo, recv = refs[:3]
    blocks = refs[3 : 3 + n]
    gain, taps, scale, ids_v, sub_out, act_own, act_send = refs[3 + n : 10 + n]
    mels, ws, wf, sub, normed, xs, idb, tmp, act, sem_in, sem_out = refs[10 + n :]
    c, z, xl = meta[0], meta[1], meta[2]
    span = own.shape[0]
    rows = mels.shape[0]
    width = sub.shape[1]
    hw = act.shape[1]
    sr = ws.shape[0] // 16
    fr = wf.shape[0] // 16

    mine = pl.multiple_of(HALF + span * c, HALF)
    other = pl.multiple_of(HALF + span * (1 - c), HALF)
    outer = pl.multiple_of((rows - HALF) * c, HALF)
    inner = pl.multiple_of((rows - HALF) * (1 - c), HALF)
    copies = [
        pltpu.make_async_copy(own, mels.at[pl.ds(mine, span)], sem_in.at[0]),
        pltpu.make_async_copy(recv.at[pl.ds(0, span)], mels.at[pl.ds(other, span)], sem_in.at[1]),
        pltpu.make_async_copy(halo, mels.at[pl.ds(outer, HALF)], sem_in.at[2]),
        pltpu.make_async_copy(recv.at[pl.ds(span, HALF)], mels.at[pl.ds(inner, HALF)], sem_in.at[3]),
    ]
    late = []
    at = 4
    for which, base, flip, shift, lo, hi in places:
        block = blocks[which]
        xx = (1 - xl) if flip else xl
        j = xx * 8 + lax.rem(z + shift + 8, 8)
        if lo < sr:
            copies.append(
                pltpu.make_async_copy(
                    block.at[pl.ds(base, sr)],
                    ws.at[pl.ds(pl.multiple_of(j * sr, sr), sr)],
                    sem_in.at[at],
                )
            )
            at += 1
        a, b = max(lo, sr), hi
        late.append(
            pltpu.make_async_copy(
                block.at[pl.ds(base + a - lo, b - a)],
                wf.at[pl.ds(pl.multiple_of(j * fr + (a - sr), 32), b - a)],
                sem_in.at[at],
            )
        )
        at += 1
    for cp in copies + late:
        cp.start()
    idb[...] = jnp.broadcast_to(ids_v[...], idb.shape)
    for cp in copies:
        cp.wait()

    steps = 8
    chunk = 2 * span // steps
    tail = rows - HALF

    def embed(i):
        r = pl.ds(pl.multiple_of(HALF + i * chunk, HALF), chunk)
        sub[r, :] = jnp.dot(mels[r, :], ws[...], preferred_element_type=jnp.float32).astype(
            jnp.bfloat16
        )

    def norm16(at):
        r = pl.ds(pl.multiple_of(at, HALF), HALF)
        f = sub[r, :].astype(jnp.float32)
        mean = jnp.sum(f, axis=1, keepdims=True) * (1.0 / width)
        d = f - mean
        var = jnp.sum(d * d, axis=1, keepdims=True) * (1.0 / width)
        normed[r, :] = (d * lax.rsqrt(var + 1e-05) * gain[...]).astype(jnp.bfloat16)

    def norm(i):
        for q in range(chunk // HALF):
            norm16(HALF + i * chunk + q * HALF)

    ends = jnp.concatenate([mels[0:HALF, :], mels[tail:, :]])
    s = jnp.dot(ends, ws[...], preferred_element_type=jnp.float32).astype(jnp.bfloat16)
    sub[0:HALF, :] = s[:HALF]
    sub[tail:, :] = s[HALF:]
    embed(0)
    norm16(0)
    norm16(tail)

    def front(i, _):
        embed(i)
        norm(i - 1)
        return 0

    lax.fori_loop(1, steps, front, 0)
    norm(steps - 1)
    out_sub = pltpu.make_async_copy(sub.at[pl.ds(mine, span)], sub_out, sem_out.at[0])
    out_sub.start()
    for cp in late:
        cp.wait()

    def gated(lhs, cg):
        vcol, gcol = cg * 256, hw + cg * 256
        v = jnp.dot(lhs, wf[:, vcol : vcol + 256], preferred_element_type=jnp.float32)
        g = jnp.dot(lhs, wf[:, gcol : gcol + 256], preferred_element_type=jnp.float32)
        return (v * jax.nn.sigmoid(g)).astype(jnp.bfloat16).astype(jnp.float32)

    def edges(cg):
        glu = gated(jnp.concatenate([normed[0:HALF, :], normed[tail:, :]]), cg)
        for h in range(2):
            part = glu[:, h * 128 : (h + 1) * 128]
            xs[2 * cg + h, 0:HALF, :] = part[:HALF]
            xs[2 * cg + h, tail:, :] = part[HALF:]

    def project(i, cg):
        r = pl.ds(pl.multiple_of(HALF + i * chunk, HALF), chunk)
        glu = gated(normed[r, :], cg)
        for h in range(2):
            xs[2 * cg + h, r, :] = glu[:, h * 128 : (h + 1) * 128]

    win = TILE + KW

    def conv(g, t0, u, buf):
        buf[...] = jnp.where(idb[pl.ds(t0, win), :] == u, xs[g, pl.ds(t0, win), :], 0.0)
        s = None
        for b in range(8):
            y = buf[b : b + TILE + KW - 8, :]
            for a in range(KW // 8):
                k = 8 * a + b
                term = y[8 * a : 8 * a + TILE].reshape(TILE // 8, 8, 128) * taps[g, k][None]
                s = term if s is None else s + term
        v = s.reshape(TILE, 128) * scale[:, g * 128 : (g + 1) * 128]
        return (v * jax.nn.sigmoid(v)).astype(jnp.bfloat16)

    def tiles(i, cg):
        for q in range(chunk // TILE):
            t0 = pl.multiple_of(i * chunk + q * TILE, TILE)
            for g in (2 * cg, 2 * cg + 1):
                act[pl.ds(t0, TILE), g * 128 : (g + 1) * 128] = conv(
                    g, t0, ids_s[t0 + HALF], tmp.at[(2 * q + g) % 4]
                )

        def again(u, _):
            t0 = pl.multiple_of(jnp.bitwise_and(starts[u], -TILE), TILE)
            keep = idb[pl.ds(pl.multiple_of(t0 + HALF, HALF), TILE), :] == u
            for g in (2 * cg, 2 * cg + 1):
                cols = slice(g * 128, (g + 1) * 128)
                new = conv(g, t0, u, tmp.at[g % 4]).astype(jnp.float32)
                old = act[pl.ds(t0, TILE), cols].astype(jnp.float32)
                act[pl.ds(t0, TILE), cols] = jnp.where(keep, new, old).astype(jnp.bfloat16)
            return 0

        row = i * chunk + HALF
        lax.fori_loop(ids_s[row] + 1, ids_s[row + chunk - 1] + 1, again, 0)

    groups = hw // 256
    for cg in range(groups):
        edges(cg)

    def lead(i, _):
        project(i, 0)
        return 0

    lax.fori_loop(0, steps, lead, 0)
    for cg in range(groups):

        def both(i, _):
            if cg + 1 < groups:
                project(i, cg + 1)
            tiles(i, cg)
            return 0

        lax.fori_loop(0, steps, both, 0)

    outs = [
        pltpu.make_async_copy(
            act.at[pl.ds(pl.multiple_of(span * c, span), span)], act_own, sem_out.at[1]
        ),
        pltpu.make_async_copy(
            act.at[pl.ds(pl.multiple_of(span * (1 - c), span), span)], act_send, sem_out.at[2]
        ),
    ]
    for cp in outs:
        cp.start()
    out_sub.wait()
    for cp in outs:
        cp.wait()


def back_kernel(meta, sub, mine, theirs, w, out, sub_v, a_v, w_v, o_v, sem_in, sem_out):
    c = meta[0]
    span, width = sub.shape
    hw = mine.shape[1]
    here = pl.multiple_of(hw * c, 128)
    there = pl.multiple_of(hw * (1 - c), 128)
    acts = [
        pltpu.make_async_copy(mine, a_v.at[:, pl.ds(here, hw)], sem_in.at[0]),
        pltpu.make_async_copy(theirs, a_v.at[:, pl.ds(there, hw)], sem_in.at[1]),
    ]
    parts = [pltpu.make_async_copy(w.at[:, h], w_v.at[h], sem_in.at[2 + h]) for h in range(2)]
    base = pltpu.make_async_copy(sub, sub_v, sem_in.at[4])
    for cp in [parts[0]] + acts + [base, parts[1]]:
        cp.start()
    for cp in acts:
        cp.wait()
    nb = 256
    outs = []
    for h in range(2):
        parts[h].wait()
        if h == 0:
            base.wait()
        for i in range(span // nb):
            r = pl.ds(i * nb, nb)
            for n in range(0, hw, 256):
                rhs = w_v[h, :, :, n : n + 256].reshape(width, 256)
                y = jnp.dot(a_v[r, :], rhs, preferred_element_type=jnp.float32)
                to = slice(h * hw + n, h * hw + n + 256)
                o_v[r, to] = (sub_v[r, to].astype(jnp.float32) + y).astype(jnp.bfloat16)
            cols = pl.ds(h * hw, hw)
            outs.append(pltpu.make_async_copy(o_v.at[r, cols], out.at[r, cols], sem_out.at[len(outs)]))
            outs[-1].start()
    for cp in outs:
        cp.wait()


def on_device(mels, utt_lengths, sub_weight, norm_gain, first_weight, dw_kernel, bn_scale, second_weight):
    _, span, stack = mels.shape
    width = second_weight.shape[1]
    hw = width // 2
    sr, fr = sub_weight.shape[0], first_weight.shape[0]
    c = lax.axis_index("c")
    z = lax.axis_index("z")
    xl = lax.axis_index("xl")
    chip = lax.axis_index("y") * 2 + lax.axis_index("xh")
    barrier = lax.optimization_barrier
    zshift = lambda a, s: lax.ppermute(a, "z", cyc(8, s))
    cross = lambda a: lax.ppermute(a, ("xh", "c", "xl"), CROSS)
    swap = lambda a: lax.ppermute(a, "c", cyc(2, 1))

    half = lambda a, at: lax.dynamic_slice_in_dim(a, at + c * hw, hw, axis=a.ndim - 1)
    hi = sr + fr
    block = pl.pallas_call(
        pack_kernel,
        out_shape=jax.ShapeDtypeStruct((hi, width), jnp.bfloat16),
        in_specs=[VM] * 2,
        out_specs=VM,
        name="front_pack",
    )(sub_weight, first_weight)
    rows = 2 * span + 2 * HALF
    ends = jnp.cumsum(utt_lengths.reshape(-1))
    positions = chip * 2 * span - HALF + jnp.arange(rows, dtype=jnp.int32)
    ids = jnp.sum((positions[:, None] >= ends[None, :]).astype(jnp.int32), axis=1)
    meta = jnp.stack([c, z, xl]).astype(jnp.int32)
    starts = jnp.concatenate([jnp.zeros(1, jnp.int32), ends]) - chip * 2 * span
    taps = half(dw_kernel, 0).astype(jnp.float32).reshape(KW, hw // 128, 128).transpose(1, 0, 2)
    taps = jnp.broadcast_to(taps[:, :, None, :], (hw // 128, KW, 8, 128))
    gain = norm_gain.reshape(1, width)
    scale = half(bn_scale.reshape(1, width), 0)
    small = (meta, ids, ids.reshape(rows, 1), starts, taps, gain, scale)

    blocks, places = [], []

    own = mels.reshape(span, stack)
    edge = lax.dynamic_slice_in_dim(own, c * (span - HALF), HALF, axis=0)
    n_tm = 16
    out_pairs = [(2 * j + 1, 2 * j + 2) for j in range(n_tm // 2 - 1)]
    halo = lax.ppermute(edge, TM, out_pairs + [(b, a) for a, b in out_pairs])

    def landed(array, parts):
        at = 0
        for flip, shift, lo, up in parts:
            places.append((len(blocks), at, flip, shift, lo, up))
            at += up - lo
        blocks.append(array)

    w_half = half(second_weight, 0)
    p = m = block
    crossed = [cross(block)]
    for s in (1, 2, 3):
        p, m = zshift(p, 1), zshift(m, -1)
        if s == 1:
            p, m, small = barrier((p, m, small))
        elif s == 2:
            p, m, crossed[0] = barrier((p, m, crossed[0]))
        elif s == 3:
            p, m, crossed[1] = barrier((p, m, crossed[1]))
        landed(p, [(False, -s, 0, hi)])
        landed(m, [(False, s, 0, hi)])
        crossed.append(cross(jnp.concatenate([p, m])))
    landed(block, [(False, 0, 0, hi)])
    for s, array in enumerate(crossed):
        landed(array, [(True, -s, 0, hi), (True, s, 0, hi)] if s else [(True, 0, 0, hi)])
    landed(lax.ppermute(jnp.where(c == 0, p, m), ("xh", "c", "xl", "z"), DIAG), [(True, 4, 0, hi)])
    landed(zshift(p[: hi // 2], 1), [(False, 4, 0, hi // 2)])
    landed(zshift(m[hi // 2 :], -1), [(False, 4, hi // 2, hi)])

    recv = swap(jnp.concatenate([own, halo]))
    w_back = lax.all_gather(w_half, FS + ("c",), axis=0, tiled=True)
    w_back = w_back.reshape(16, 2, fr, hw)

    meta, ids, ids_col, starts, taps, gain, scale = small
    bf, f32 = jnp.bfloat16, jnp.float32
    n_in = 4 + 2 * len(places)
    sub, act_own, act_send = pl.pallas_call(
        functools.partial(front_kernel, places),
        out_shape=[
            jax.ShapeDtypeStruct((span, width), bf),
            jax.ShapeDtypeStruct((span, hw), bf),
            jax.ShapeDtypeStruct((span, hw), bf),
        ],
        in_specs=[SM] * 3 + [ANY] * (3 + len(blocks)) + [VM] * 4,
        out_specs=[ANY] * 3,
        scratch_shapes=[
            pltpu.VMEM((rows, stack), bf),
            pltpu.VMEM((16 * sr, width), bf),
            pltpu.VMEM((16 * fr, width), bf),
            pltpu.VMEM((rows, width), bf),
            pltpu.VMEM((rows, width), bf),
            pltpu.VMEM((hw // 128, rows, 128), f32),
            pltpu.VMEM((rows, 128), jnp.int32),
            pltpu.VMEM((4, TILE + KW, 128), f32),
            pltpu.VMEM((2 * span, hw), bf),
            pltpu.SemaphoreType.DMA((n_in,)),
            pltpu.SemaphoreType.DMA((3,)),
        ],
        compiler_params=pltpu.CompilerParams(vmem_limit_bytes=60 << 20),
        cost_estimate=pl.CostEstimate(flops=10_000_000_000, bytes_accessed=12 << 20, transcendentals=0),
        name="front",
    )(meta, ids, starts, own, halo, recv, *blocks, gain, taps, scale, ids_col)

    w_back, act_send = barrier((w_back, act_send))
    act_recv = swap(act_send)
    out = pl.pallas_call(
        back_kernel,
        out_shape=jax.ShapeDtypeStruct((span, width), bf),
        in_specs=[SM] + [ANY] * 2 + [VM] + [ANY],
        out_specs=ANY,
        scratch_shapes=[
            pltpu.VMEM((span, width), bf),
            pltpu.VMEM((span, width), bf),
            pltpu.VMEM((2, 16, fr, hw), bf),
            pltpu.VMEM((span, width), bf),
            pltpu.SemaphoreType.DMA((5,)),
            pltpu.SemaphoreType.DMA((6,)),
        ],
        compiler_params=pltpu.CompilerParams(vmem_limit_bytes=60 << 20),
        cost_estimate=pl.CostEstimate(flops=3_600_000_000, bytes_accessed=12 << 20, transcendentals=0),
        name="back",
    )(meta, sub, act_own, act_recv, w_back)
    return out.reshape(1, span, width)


def solution(mesh):
    fine = Mesh(mesh.devices.reshape(4, 2, 2, 2, 8), ("y", "xh", "c", "xl", "z"))
    in_specs = (
        P(FS, TM, None),
        P(FS, None),
        P(FS, None),
        P(),
        P(FS, None),
        P(),
        P(),
        P(FS, None),
    )
    return jax.shard_map(
        on_device, mesh=fine, in_specs=in_specs, out_specs=P(FS, TM, None), check_vma=False
    )
```

```python
import functools

import jax
import jax.numpy as jnp
from jax import lax
from jax.experimental import pallas as pl
from jax.experimental.pallas import tpu as pltpu
from jax.sharding import Mesh
from jax.sharding import PartitionSpec as P

KW = 32
HALF = KW // 2
TM = ("y", "xh", "c")
FS = ("xl", "z")
CROSS = [
    ((xh * 2 + c) * 2 + xl, ((x2 // 2) * 2 + c) * 2 + x2 % 2)
    for xh in range(2)
    for c in range(2)
    for xl in range(2)
    for x2 in [(xh * 2 + xl + (1 if c == 0 else 3)) % 4]
]
LAST = [
    ((c * 2 + xl) * 8 + z, (c * 2 + xl) * 8 + (z + (1 if c == 0 else -1)) % 8)
    for c in range(2)
    for xl in range(2)
    for z in range(8)
]
DIAG = [
    (((xh * 2 + c) * 2 + xl) * 8 + z, (((x2 // 2) * 2 + c) * 2 + x2 % 2) * 8 + (z + d) % 8)
    for xh in range(2)
    for c in range(2)
    for xl in range(2)
    for z in range(8)
    for d in [1 if c == 0 else -1]
    for x2 in [(xh * 2 + xl + d) % 4]
]
TILE = 32
ANY = pl.BlockSpec(memory_space=pl.ANY)
VM = pl.BlockSpec(memory_space=pltpu.VMEM)
SM = pl.BlockSpec(memory_space=pltpu.SMEM)


def cyc(n, s):
    return [(i, (i + s) % n) for i in range(n)]


def pack_kernel(sub, first, out):
    c = lax.axis_index("c")
    sr, width = sub.shape
    hw = width // 2
    out[0:sr, :] = sub[...]
    for h in range(2):
        cols = pl.ds(pl.multiple_of(h * width + c * hw, 128), hw)
        out[sr:, h * hw : (h + 1) * hw] = first[:, cols]


def front_kernel(places, meta, ids_s, starts, *refs):
    n = places[-1][0] + 1
    own, halo, recv = refs[:3]
    blocks = refs[3 : 3 + n]
    gain, taps, scale, ids_v, sub_out, act_own, act_send = refs[3 + n : 10 + n]
    mels, ws, wf, sub, normed, xs, idb, tmp, act, sem_in, sem_out = refs[10 + n :]
    c, z, xl = meta[0], meta[1], meta[2]
    span = own.shape[0]
    rows = mels.shape[0]
    width = sub.shape[1]
    hw = act.shape[1]
    sr = ws.shape[0] // 16
    fr = wf.shape[0] // 16

    mine = pl.multiple_of(HALF + span * c, HALF)
    other = pl.multiple_of(HALF + span * (1 - c), HALF)
    outer = pl.multiple_of((rows - HALF) * c, HALF)
    inner = pl.multiple_of((rows - HALF) * (1 - c), HALF)
    copies = [
        pltpu.make_async_copy(own, mels.at[pl.ds(mine, span)], sem_in.at[0]),
        pltpu.make_async_copy(recv.at[pl.ds(0, span)], mels.at[pl.ds(other, span)], sem_in.at[1]),
        pltpu.make_async_copy(halo, mels.at[pl.ds(outer, HALF)], sem_in.at[2]),
        pltpu.make_async_copy(recv.at[pl.ds(span, HALF)], mels.at[pl.ds(inner, HALF)], sem_in.at[3]),
    ]
    late = []
    at = 4
    for which, base, flip, shift, lo, hi in places:
        block = blocks[which]
        xx = (1 - xl) if flip else xl
        j = xx * 8 + lax.rem(z + shift + 8, 8)
        if lo < sr:
            copies.append(
                pltpu.make_async_copy(
                    block.at[pl.ds(base, sr)],
                    ws.at[pl.ds(pl.multiple_of(j * sr, sr), sr)],
                    sem_in.at[at],
                )
            )
            at += 1
        a, b = max(lo, sr), hi
        late.append(
            pltpu.make_async_copy(
                block.at[pl.ds(base + a - lo, b - a)],
                wf.at[pl.ds(pl.multiple_of(j * fr + (a - sr), 32), b - a)],
                sem_in.at[at],
            )
        )
        at += 1
    for cp in copies + late:
        cp.start()
    idb[...] = jnp.broadcast_to(ids_v[...], idb.shape)
    for cp in copies:
        cp.wait()

    steps = 8
    chunk = 2 * span // steps
    tail = rows - HALF

    def embed(i):
        r = pl.ds(pl.multiple_of(HALF + i * chunk, HALF), chunk)
        sub[r, :] = jnp.dot(mels[r, :], ws[...], preferred_element_type=jnp.float32).astype(
            jnp.bfloat16
        )

    def norm16(at):
        r = pl.ds(pl.multiple_of(at, HALF), HALF)
        f = sub[r, :].astype(jnp.float32)
        mean = jnp.sum(f, axis=1, keepdims=True) * (1.0 / width)
        d = f - mean
        var = jnp.sum(d * d, axis=1, keepdims=True) * (1.0 / width)
        normed[r, :] = (d * lax.rsqrt(var + 1e-05) * gain[...]).astype(jnp.bfloat16)

    def norm(i):
        for q in range(chunk // HALF):
            norm16(HALF + i * chunk + q * HALF)

    ends = jnp.concatenate([mels[0:HALF, :], mels[tail:, :]])
    s = jnp.dot(ends, ws[...], preferred_element_type=jnp.float32).astype(jnp.bfloat16)
    sub[0:HALF, :] = s[:HALF]
    sub[tail:, :] = s[HALF:]
    embed(0)
    norm16(0)
    norm16(tail)

    def front(i, _):
        embed(i)
        norm(i - 1)
        return 0

    lax.fori_loop(1, steps, front, 0)
    norm(steps - 1)
    out_sub = pltpu.make_async_copy(sub.at[pl.ds(mine, span)], sub_out, sem_out.at[0])
    out_sub.start()
    for cp in late:
        cp.wait()

    def gated(lhs, cg):
        vcol, gcol = cg * 256, hw + cg * 256
        v = jnp.dot(lhs, wf[:, vcol : vcol + 256], preferred_element_type=jnp.float32)
        g = jnp.dot(lhs, wf[:, gcol : gcol + 256], preferred_element_type=jnp.float32)
        return (v * jax.nn.sigmoid(g)).astype(jnp.bfloat16).astype(jnp.float32)

    def edges(cg):
        glu = gated(jnp.concatenate([normed[0:HALF, :], normed[tail:, :]]), cg)
        for h in range(2):
            part = glu[:, h * 128 : (h + 1) * 128]
            xs[2 * cg + h, 0:HALF, :] = part[:HALF]
            xs[2 * cg + h, tail:, :] = part[HALF:]

    def project(i, cg):
        r = pl.ds(pl.multiple_of(HALF + i * chunk, HALF), chunk)
        glu = gated(normed[r, :], cg)
        for h in range(2):
            xs[2 * cg + h, r, :] = glu[:, h * 128 : (h + 1) * 128]

    win = TILE + KW

    def conv(g, t0, u, buf):
        buf[...] = jnp.where(idb[pl.ds(t0, win), :] == u, xs[g, pl.ds(t0, win), :], 0.0)
        s = None
        for b in range(8):
            y = buf[b : b + TILE + KW - 8, :]
            for a in range(KW // 8):
                k = 8 * a + b
                term = y[8 * a : 8 * a + TILE].reshape(TILE // 8, 8, 128) * taps[g, k][None]
                s = term if s is None else s + term
        v = s.reshape(TILE, 128) * scale[:, g * 128 : (g + 1) * 128]
        return (v * jax.nn.sigmoid(v)).astype(jnp.bfloat16)

    def tiles(i, cg):
        for q in range(chunk // TILE):
            t0 = pl.multiple_of(i * chunk + q * TILE, TILE)
            for g in (2 * cg, 2 * cg + 1):
                act[pl.ds(t0, TILE), g * 128 : (g + 1) * 128] = conv(
                    g, t0, ids_s[t0 + HALF], tmp.at[(2 * q + g) % 4]
                )

        def again(u, _):
            t0 = pl.multiple_of(jnp.bitwise_and(starts[u], -TILE), TILE)
            keep = idb[pl.ds(pl.multiple_of(t0 + HALF, HALF), TILE), :] == u
            for g in (2 * cg, 2 * cg + 1):
                cols = slice(g * 128, (g + 1) * 128)
                new = conv(g, t0, u, tmp.at[g % 4]).astype(jnp.float32)
                old = act[pl.ds(t0, TILE), cols].astype(jnp.float32)
                act[pl.ds(t0, TILE), cols] = jnp.where(keep, new, old).astype(jnp.bfloat16)
            return 0

        row = i * chunk + HALF
        lax.fori_loop(ids_s[row] + 1, ids_s[row + chunk - 1] + 1, again, 0)

    groups = hw // 256
    for cg in range(groups):
        edges(cg)

    def lead(i, _):
        project(i, 0)
        return 0

    lax.fori_loop(0, steps, lead, 0)
    for cg in range(groups):

        def both(i, _):
            if cg + 1 < groups:
                project(i, cg + 1)
            tiles(i, cg)
            return 0

        lax.fori_loop(0, steps, both, 0)

    outs = [
        pltpu.make_async_copy(
            act.at[pl.ds(pl.multiple_of(span * c, span), span)], act_own, sem_out.at[1]
        ),
        pltpu.make_async_copy(
            act.at[pl.ds(pl.multiple_of(span * (1 - c), span), span)], act_send, sem_out.at[2]
        ),
    ]
    for cp in outs:
        cp.start()
    out_sub.wait()
    for cp in outs:
        cp.wait()


def back_kernel(meta, sub, mine, theirs, w, out, sub_v, a_v, w_v, o_v, sem_in, sem_out):
    c = meta[0]
    span, width = sub.shape
    hw = mine.shape[1]
    here = pl.multiple_of(hw * c, 128)
    there = pl.multiple_of(hw * (1 - c), 128)
    acts = [
        pltpu.make_async_copy(mine, a_v.at[:, pl.ds(here, hw)], sem_in.at[0]),
        pltpu.make_async_copy(theirs, a_v.at[:, pl.ds(there, hw)], sem_in.at[1]),
    ]
    parts = [pltpu.make_async_copy(w.at[:, h], w_v.at[h], sem_in.at[2 + h]) for h in range(2)]
    base = pltpu.make_async_copy(sub, sub_v, sem_in.at[4])
    for cp in [parts[0]] + acts + [base, parts[1]]:
        cp.start()
    for cp in acts:
        cp.wait()
    nb = 256
    outs = []
    for h in range(2):
        parts[h].wait()
        if h == 0:
            base.wait()
        for i in range(span // nb):
            r = pl.ds(i * nb, nb)
            for n in range(0, hw, 256):
                rhs = w_v[h, :, :, n : n + 256].reshape(width, 256)
                y = jnp.dot(a_v[r, :], rhs, preferred_element_type=jnp.float32)
                to = slice(h * hw + n, h * hw + n + 256)
                o_v[r, to] = (sub_v[r, to].astype(jnp.float32) + y).astype(jnp.bfloat16)
            cols = pl.ds(h * hw, hw)
            outs.append(pltpu.make_async_copy(o_v.at[r, cols], out.at[r, cols], sem_out.at[len(outs)]))
            outs[-1].start()
    for cp in outs:
        cp.wait()


def on_device(mels, utt_lengths, sub_weight, norm_gain, first_weight, dw_kernel, bn_scale, second_weight):
    _, span, stack = mels.shape
    width = second_weight.shape[1]
    hw = width // 2
    sr, fr = sub_weight.shape[0], first_weight.shape[0]
    c = lax.axis_index("c")
    z = lax.axis_index("z")
    xl = lax.axis_index("xl")
    chip = lax.axis_index("y") * 2 + lax.axis_index("xh")
    barrier = lax.optimization_barrier
    zshift = lambda a, s: lax.ppermute(a, "z", cyc(8, s))
    cross = lambda a: lax.ppermute(a, ("xh", "c", "xl"), CROSS)
    swap = lambda a: lax.ppermute(a, "c", cyc(2, 1))

    half = lambda a, at: lax.dynamic_slice_in_dim(a, at + c * hw, hw, axis=a.ndim - 1)
    hi = sr + fr
    block = pl.pallas_call(
        pack_kernel,
        out_shape=jax.ShapeDtypeStruct((hi, width), jnp.bfloat16),
        in_specs=[VM] * 2,
        out_specs=VM,
        name="front_pack",
    )(sub_weight, first_weight)
    rows = 2 * span + 2 * HALF
    ends = jnp.cumsum(utt_lengths.reshape(-1))
    positions = chip * 2 * span - HALF + jnp.arange(rows, dtype=jnp.int32)
    ids = jnp.sum((positions[:, None] >= ends[None, :]).astype(jnp.int32), axis=1)
    meta = jnp.stack([c, z, xl]).astype(jnp.int32)
    starts = jnp.concatenate([jnp.zeros(1, jnp.int32), ends]) - chip * 2 * span
    taps = half(dw_kernel, 0).astype(jnp.float32).reshape(KW, hw // 128, 128).transpose(1, 0, 2)
    taps = jnp.broadcast_to(taps[:, :, None, :], (hw // 128, KW, 8, 128))
    gain = norm_gain.reshape(1, width)
    scale = half(bn_scale.reshape(1, width), 0)
    small = (meta, ids, ids.reshape(rows, 1), starts, taps, gain, scale)

    blocks, places = [], []

    own = mels.reshape(span, stack)
    edge = lax.dynamic_slice_in_dim(own, c * (span - HALF), HALF, axis=0)
    n_tm = 16
    out_pairs = [(2 * j + 1, 2 * j + 2) for j in range(n_tm // 2 - 1)]
    halo = lax.ppermute(edge, TM, out_pairs + [(b, a) for a, b in out_pairs])

    def landed(array, parts):
        at = 0
        for flip, shift, lo, up in parts:
            places.append((len(blocks), at, flip, shift, lo, up))
            at += up - lo
        blocks.append(array)

    w_half = half(second_weight, 0)
    p = m = block
    crossed = [cross(block)]
    for s in (1, 2, 3):
        p, m = zshift(p, 1), zshift(m, -1)
        if s == 1:
            p, m, small = barrier((p, m, small))
        elif s == 2:
            p, m, crossed[0] = barrier((p, m, crossed[0]))
        elif s == 3:
            p, m, crossed[1] = barrier((p, m, crossed[1]))
        landed(p, [(False, -s, 0, hi)])
        landed(m, [(False, s, 0, hi)])
        crossed.append(cross(jnp.concatenate([p, m])))
    landed(block, [(False, 0, 0, hi)])
    for s, array in enumerate(crossed):
        landed(array, [(True, -s, 0, hi), (True, s, 0, hi)] if s else [(True, 0, 0, hi)])
    opposite = jnp.where(c == 0, p, m)
    landed(lax.ppermute(opposite, ("c", "xl", "z"), LAST), [(False, 4, 0, hi)])
    landed(lax.ppermute(opposite, ("xh", "c", "xl", "z"), DIAG), [(True, 4, 0, hi)])

    recv = swap(jnp.concatenate([own, halo]))
    w_back = lax.all_gather(w_half, FS + ("c",), axis=0, tiled=True)
    w_back = w_back.reshape(16, 2, fr, hw)

    meta, ids, ids_col, starts, taps, gain, scale = small
    bf, f32 = jnp.bfloat16, jnp.float32
    n_in = 4 + 2 * len(places)
    sub, act_own, act_send = pl.pallas_call(
        functools.partial(front_kernel, places),
        out_shape=[
            jax.ShapeDtypeStruct((span, width), bf),
            jax.ShapeDtypeStruct((span, hw), bf),
            jax.ShapeDtypeStruct((span, hw), bf),
        ],
        in_specs=[SM] * 3 + [ANY] * (3 + len(blocks)) + [VM] * 4,
        out_specs=[ANY] * 3,
        scratch_shapes=[
            pltpu.VMEM((rows, stack), bf),
            pltpu.VMEM((16 * sr, width), bf),
            pltpu.VMEM((16 * fr, width), bf),
            pltpu.VMEM((rows, width), bf),
            pltpu.VMEM((rows, width), bf),
            pltpu.VMEM((hw // 128, rows, 128), f32),
            pltpu.VMEM((rows, 128), jnp.int32),
            pltpu.VMEM((4, TILE + KW, 128), f32),
            pltpu.VMEM((2 * span, hw), bf),
            pltpu.SemaphoreType.DMA((n_in,)),
            pltpu.SemaphoreType.DMA((3,)),
        ],
        compiler_params=pltpu.CompilerParams(vmem_limit_bytes=60 << 20),
        cost_estimate=pl.CostEstimate(flops=10_000_000_000, bytes_accessed=12 << 20, transcendentals=0),
        name="front",
    )(meta, ids, starts, own, halo, recv, *blocks, gain, taps, scale, ids_col)

    w_back, act_send = barrier((w_back, act_send))
    act_recv = swap(act_send)
    out = pl.pallas_call(
        back_kernel,
        out_shape=jax.ShapeDtypeStruct((span, width), bf),
        in_specs=[SM] + [ANY] * 2 + [VM] + [ANY],
        out_specs=ANY,
        scratch_shapes=[
            pltpu.VMEM((span, width), bf),
            pltpu.VMEM((span, width), bf),
            pltpu.VMEM((2, 16, fr, hw), bf),
            pltpu.VMEM((span, width), bf),
            pltpu.SemaphoreType.DMA((5,)),
            pltpu.SemaphoreType.DMA((6,)),
        ],
        compiler_params=pltpu.CompilerParams(vmem_limit_bytes=60 << 20),
        cost_estimate=pl.CostEstimate(flops=3_600_000_000, bytes_accessed=12 << 20, transcendentals=0),
        name="back",
    )(meta, sub, act_own, act_recv, w_back)
    return out.reshape(1, span, width)


def solution(mesh):
    fine = Mesh(mesh.devices.reshape(4, 2, 2, 2, 8), ("y", "xh", "c", "xl", "z"))
    in_specs = (
        P(FS, TM, None),
        P(FS, None),
        P(FS, None),
        P(),
        P(FS, None),
        P(),
        P(),
        P(FS, None),
    )
    return jax.shard_map(
        on_device, mesh=fine, in_specs=in_specs, out_specs=P(FS, TM, None), check_vma=False
    )
```
